128 devices in a mesh: agent: 8 (over z, core), chan: 8 (over y, x_hi), batch: 2 (over x_lo).
Axes of the slice: x: 4 (x_hi: 2, x_lo: 2; x = x_hi * 2 + x_lo), y: 4, z: 4, core: 2. Of those that a mesh axis runs over, the one named last changes fastest.
Arguments:
- features: bfloat16 [256, 16, 16384], P(None, None, ('agent', 'chan', 'batch')), may hold values from -6 to 6
- norm_gain: float32 [256], replicated, may hold values from 0.1 to 1.9
- tok_in: bfloat16 [16384, 2048], P('agent'), may hold values from -0.046875 to 0.046875
- tok_out: bfloat16 [2048, 16384], P(None, 'agent'), may hold values from -0.125 to 0.125
- mix_gain: float32 [256], replicated, may hold values from 0.1 to 1.9
- chan_in: bfloat16 [256, 1024], replicated, may hold values from -0.375 to 0.375
- chan_out: bfloat16 [1024, 256], replicated, may hold values from -0.1875 to 0.1875
- head: bfloat16 [256, 8], replicated, may hold values from -8 to 8
- actions: int32 [16, 16384], P(None, ('agent', 'chan', 'batch')), may hold values from 0 to 7
- order: int32 [16384], P(('agent', 'chan', 'batch')), may hold values from 0 to 16383, as said below
Outputs:
- input_grad: float32 [256, 16, 16384], P(None, None, ('agent', 'chan', 'batch'))
- head_grad: float32 [256, 8], replicated
The draws below stay inside these ranges and needn't reach their ends.
Inputs may be any that keep to these rules, and one draw needn't show every extreme that they name: order maps each aligned block of 128 agents one to one onto the same block.
All inputs are finite; a program needn't handle non-finite values.
Results may differ from the reference program's by a relative error of at most 0.025.
Values may be sent and summed in bfloat16 or wider, within the bound.
A program may use at most 128 MiB of HBM per device.

```python
import jax
import jax.numpy as jnp
from jax import lax

A = 16384
TH = 2048
C = 256
CH = 1024
P_SIZE = 8
SAMPLES = 16
A_LOC = 128


def draw_head(key, part):
    base = jnp.clip(jax.random.normal(key, (C, P_SIZE), jnp.float32), -4.0, 4.0)
    return (base * C ** (-0.5)).astype(jnp.bfloat16)


def block_order(key):
    return jax.random.permutation(key, A_LOC).astype(jnp.int32)


def draw_order(key, part):
    blocks = A // A_LOC
    keys = jax.random.split(key, blocks)
    perms = jax.vmap(block_order)(keys)
    starts = jnp.arange(blocks, dtype=jnp.int32)[:, None] * A_LOC
    return (perms + starts).reshape(A)


def plant(entries, key, least, largest):
    shape = entries.shape
    index_at = [jax.random.randint(jax.random.fold_in(key, axis), (), 0, shape[axis]) for axis in range(len(shape))]
    entries = entries.at[tuple(index_at)].set(least)
    longest = shape.index(max(shape))
    index_at[longest] = (index_at[longest] + 1) % shape[longest]
    return entries.at[tuple(index_at)].set(largest)


def block_levels(stream_key, dims, cuts, low, top_value):
    def one(axis_at, parts):
        heights = jax.random.uniform(jax.random.fold_in(jax.random.fold_in(stream_key, 6), axis_at), (parts,), jnp.float32, low / len(cuts), top_value / len(cuts))
        return jnp.repeat(jnp.exp(heights), dims[axis_at] // parts).reshape((-1,) + (1,) * (len(dims) - axis_at - 1))

    factor_of = one(*cuts[0])
    for cut in cuts[1:]:
        factor_of = factor_of * one(*cut)
    return factor_of


def bell_draw(rng, dims, width, limit, cuts=(), kind=jnp.bfloat16):
    array = jax.random.normal(rng, dims, jnp.float32) * width
    if len(cuts) > 0:
        array = block_levels(rng, dims, cuts, -0.22, 0.18) * array
    return jnp.clip(array, min=-limit, max=limit).astype(kind)


def setup_inputs(seed: int = 0) -> dict:
    key_list = jax.random.split(jax.random.key(seed), 11)
    features = bell_draw(key_list[0], (C, SAMPLES, A), 1.0, 6.0, ((2, 128),))
    norm_gain = jnp.clip(1.0 + 0.18 * jax.random.normal(key_list[1], (C,), jnp.float32), 0.1, 1.9)
    tok_in = bell_draw(key_list[2], (A, TH), A ** -0.5, 0.046875, ((0, 8),))
    tok_out = bell_draw(key_list[3], (TH, A), TH ** -0.5, 0.125, ((1, 8),))
    mix_gain = jnp.clip(1.0 + 0.18 * jax.random.normal(key_list[4], (C,), jnp.float32), 0.1, 1.9)
    chan_in = bell_draw(key_list[5], (C, CH), C ** -0.5, 0.375)
    chan_out = bell_draw(key_list[6], (CH, C), CH ** -0.5, 0.1875)
    head = draw_head(jax.random.fold_in(key_list[10], 71), 0)
    actions = plant(jax.random.randint(key_list[8], (SAMPLES, A), 0, P_SIZE), jax.random.fold_in(key_list[8], 1), 0, P_SIZE - 1).astype(jnp.int32)
    order = draw_order(jax.random.fold_in(key_list[10], 71), 0)
    return dict(features=features, norm_gain=norm_gain, tok_in=tok_in, tok_out=tok_out, mix_gain=mix_gain, chan_in=chan_in, chan_out=chan_out, head=head, actions=actions, order=order)


GELU_K = 0.7978845608028654
GELU_C = 0.044715
EPS = 1e-05

def gelu_value(v):
    return 0.5 * v * (1.0 + jnp.tanh(GELU_K * (v + GELU_C * v * v * v)))

def gelu_slope(v):
    inner = jnp.tanh(GELU_K * (v + GELU_C * v * v * v))
    return 0.5 * (1.0 + inner) + 0.5 * v * (1.0 - inner * inner) * GELU_K * (1.0 + 3.0 * GELU_C * v * v)

def shaped_gain(gain, field):
    return gain.reshape((gain.shape[0],) + (1,) * (field.ndim - 1))

def norm_forward(field, gain):
    center = lax.optimization_barrier(jnp.mean(field, axis=0, keepdims=True))
    spread = lax.optimization_barrier(jnp.mean(jnp.square(field - center), axis=0, keepdims=True))
    scale = lax.rsqrt(spread + EPS)
    unit = (field - center) * scale
    return (unit * shaped_gain(gain, field), unit, scale)

def norm_backward(upstream, gain, unit, scale):
    weighted = upstream * shaped_gain(gain, upstream)
    return scale * (weighted - lax.optimization_barrier(jnp.mean(weighted, axis=0, keepdims=True)) - unit * lax.optimization_barrier(jnp.mean(weighted * unit, axis=0, keepdims=True)))

def reference(features, norm_gain, tok_in, tok_out, mix_gain, chan_in, chan_out, head, actions, order):
    wide = features.astype(jnp.float32)
    normed_in, unit_in, scale_in = norm_forward(wide, norm_gain)
    rows = normed_in.astype(jnp.bfloat16).reshape(C * SAMPLES, A)
    hidden_pre = lax.dot_general(tok_in, rows, (((0,), (1,)), ((), ())), preferred_element_type=jnp.float32)
    hidden_act = gelu_value(hidden_pre).astype(jnp.bfloat16)
    mixed = lax.dot_general(hidden_act, tok_out, (((0,), (0,)), ((), ())), preferred_element_type=jnp.float32)
    mixed = mixed.astype(jnp.bfloat16).reshape(C, SAMPLES, A)
    first = wide + mixed.astype(jnp.float32)
    target = actions[:, order].astype(jnp.int32)

    def channel_part(pair):
        field, chosen = pair
        normed_mid, unit_mid, scale_mid = norm_forward(field, mix_gain)
        inner_pre = jnp.dot(chan_in.T, normed_mid.astype(jnp.bfloat16), preferred_element_type=jnp.float32)
        inner = gelu_value(inner_pre).astype(jnp.bfloat16)
        outer = jnp.dot(chan_out.T, inner, preferred_element_type=jnp.float32)
        second = (field + outer).astype(jnp.bfloat16)
        logits = jnp.dot(head.T, second, preferred_element_type=jnp.float32)
        phases = lax.broadcasted_iota(jnp.int32, logits.shape, 0)
        picked = (phases == chosen[None, :]).astype(jnp.float32)
        top = lax.optimization_barrier(jnp.max(logits, axis=0, keepdims=True))
        exps = jnp.exp(logits - top)
        probs = exps / lax.optimization_barrier(jnp.sum(exps, axis=0, keepdims=True))
        slope = (probs - picked).astype(jnp.bfloat16)
        head_part = jnp.dot(second, slope.T, preferred_element_type=jnp.float32)
        back_second = jnp.dot(head, slope, preferred_element_type=jnp.float32)
        back_low = back_second.astype(jnp.bfloat16)
        back_inner = jnp.dot(chan_out, back_low, preferred_element_type=jnp.float32)
        back_inner_pre = (back_inner * gelu_slope(inner_pre)).astype(jnp.bfloat16)
        back_mid = jnp.dot(chan_in, back_inner_pre, preferred_element_type=jnp.float32)
        back_first = back_second + norm_backward(back_mid, mix_gain, unit_mid, scale_mid)
        return (back_first, head_part)
    back_first, head_parts = lax.map(channel_part, (jnp.transpose(first, (1, 0, 2)), target))
    back_first = jnp.transpose(back_first, (1, 0, 2))
    head_grad = lax.optimization_barrier(jnp.sum(head_parts, axis=0)) * (1.0 / (SAMPLES * A))
    back_rows = back_first.astype(jnp.bfloat16).reshape(C * SAMPLES, A)
    back_hidden = lax.dot_general(tok_out, back_rows, (((1,), (1,)), ((), ())), preferred_element_type=jnp.float32)
    back_hidden_pre = (back_hidden * gelu_slope(hidden_pre)).astype(jnp.bfloat16)
    back_norm = lax.dot_general(back_hidden_pre, tok_in, (((0,), (1,)), ((), ())), preferred_element_type=jnp.float32)
    back_norm = back_norm.astype(jnp.bfloat16).reshape(C, SAMPLES, A)
    input_grad = back_first + norm_backward(back_norm.astype(jnp.float32), norm_gain, unit_in, scale_in)
    return (input_grad, head_grad)
```

```python
import jax
import jax.numpy as jnp
from jax import lax
from jax.experimental import pallas as pl
from jax.experimental.pallas import tpu as pltpu
from jax.sharding import PartitionSpec as P

MESH = pl.DeviceIdType.MESH
F32 = jnp.float32
BF16 = jnp.bfloat16

A = 16384
B = 16
C = 256
L = 128
NP = 16
CL = C // NP
T = NP * L
J = 2048
K = 1024
NC = 2
NB = B // NC
R = NB * CL
Q = J // 8

GELU_K = 0.7978845608028654
GELU_C = 0.044715
EPS = 1e-05


def mm(a, b):
    return lax.dot_general(a, b, (((1,), (0,)), ((), ())), preferred_element_type=F32)


def mm_nt(a, b):
    return lax.dot_general(a, b, (((1,), (1,)), ((), ())), preferred_element_type=F32)


def gelu_both(v):
    square = v * v
    inner = jnp.tanh(v * (GELU_K + (GELU_K * GELU_C) * square))
    half = 0.5 + 0.5 * inner
    value = v * half
    slope = half + (0.5 * v) * (1.0 - inner * inner) * (GELU_K + (3.0 * GELU_K * GELU_C) * square)
    return value, slope


def mean0(v):
    return jnp.sum(v, axis=0, keepdims=True) * (1.0 / C)


def kernel(
    x_hbm, gin_ref, win_hbm, wout_hbm, gmid_ref, ci_hbm, co_hbm, head_ref, act_ref, ord_ref,
    out_hbm, hg_ref,
    x_s, win, wout, ci, co, cit, cot, gin, gmid, head16, headc, tgt, mu, rstd, bf,
    send1, send2, send3, send4, recv1, recv2, recv3, recv4,
    part1, part2, sibr1, sibr2, zs1, zs2, zr1, zr2, hact1, hact2, ownp, hslope,
    inner_s, slope_s, bip_s, hp, hbuf_a, hbuf_y, hbuf_x, hsend,
    ld_sem, out_sem, a2a_s, a2a_r, sib_s, sib_r, z_s, z_r, ag_s, ag_r, fw_s, fw_r,
    ha_s, ha_r, hy_s, hy_r, hx_s, hx_r,
):
    ag = lax.axis_index("agent")
    chan = lax.axis_index("chan")
    batch = lax.axis_index("batch")
    me = chan * 2 + batch
    z = ag // 2
    core = lax.rem(ag, 2)
    y = me // 4
    xx = lax.rem(me, 4)
    mine = core * 4 + z

    def plane(p):
        return {"agent": ag, "chan": p // 2, "batch": lax.rem(p, 2)}

    def line(zz, cc):
        return {"agent": zz * 2 + cc, "chan": chan, "batch": batch}

    def xor(a, d):
        out = a
        if d & 1:
            out = out + 1 - 2 * lax.rem(out, 2)
        if d & 2:
            out = lax.rem(out + 2, 4)
        return out

    loads = [
        pltpu.make_async_copy(x_hbm, x_s, ld_sem.at[0]),
        pltpu.make_async_copy(win_hbm, win, ld_sem.at[1]),
        pltpu.make_async_copy(ci_hbm, ci, ld_sem.at[2]),
        pltpu.make_async_copy(co_hbm, co, ld_sem.at[3]),
        pltpu.make_async_copy(wout_hbm, wout, ld_sem.at[4]),
    ]
    for load in loads:
        load.start()

    barrier = pltpu.get_barrier_semaphore()
    for i in range(1, NP):
        pl.semaphore_signal(barrier, inc=1, device_id=plane(lax.rem(me + i, NP)), device_id_type=MESH)
    for i in range(1, 8):
        pl.semaphore_signal(
            barrier, inc=1,
            device_id={"agent": lax.rem(ag + i, 8), "chan": chan, "batch": batch},
            device_id_type=MESH,
        )

    gin[...] = jnp.transpose(jnp.broadcast_to(gin_ref[...], (L, C)))
    gmid[...] = jnp.transpose(jnp.broadcast_to(gmid_ref[...], (L, C)))
    head_rows = jnp.concatenate([head_ref[...].astype(F32), jnp.zeros((8, C), F32)], axis=0)
    head16[...] = head_rows.astype(BF16)
    wide_head = jnp.concatenate([head_rows, jnp.zeros((L - 16, C), F32)], axis=0)
    headc[...] = jnp.transpose(wide_head)[:, :16].astype(BF16)
    spot = lax.broadcasted_iota(jnp.int32, (L, L), 0) == lax.rem(ord_ref[...], L)
    targets = mm(act_ref[...].astype(F32).astype(BF16), spot.astype(F32).astype(BF16))
    for b in range(B):
        tgt[b] = targets[b : b + 1, :]
    hp[...] = jnp.zeros((16, C), F32)

    def a2a_copy(k, h, send, recv, p, slot):
        return pltpu.make_async_remote_copy(
            src_ref=send.at[p, pl.ds(h * NB, NB)],
            dst_ref=recv.at[h, slot],
            send_sem=a2a_s.at[k, h, p],
            recv_sem=a2a_r.at[k, h, slot],
            device_id=plane(p),
            device_id_type=MESH,
        )

    def a2a_send(k, h, send, recv):
        def body(i, carry):
            a2a_copy(k, h, send, recv, lax.rem(me + i, NP), me).start()
            return carry

        lax.fori_loop(1, NP, body, 0)

    def a2a_wait(k, h, send, recv):
        recv[h, me] = send[me, pl.ds(h * NB, NB)]

        def body(i, carry):
            p = lax.rem(me + i, NP)
            a2a_copy(k, h, send, recv, p, p).wait_recv()
            return carry

        lax.fori_loop(1, NP, body, 0)

    def a2a_drain(k, h, send, recv):
        def body(i, carry):
            a2a_copy(k, h, send, recv, lax.rem(me + i, NP), me).wait_send()
            return carry

        lax.fori_loop(1, NP, body, 0)

    def sib_copy(s, h, part, sibr, i):
        return pltpu.make_async_remote_copy(
            src_ref=part.at[h, i], dst_ref=sibr.at[h, i],
            send_sem=sib_s.at[s, h, i], recv_sem=sib_r.at[s, h, i],
            device_id=line(z, 1 - core), device_id_type=MESH,
        )

    def z_copy(s, h, zs, zr, src, zz, slot):
        return pltpu.make_async_remote_copy(
            src_ref=zs.at[h, src], dst_ref=zr.at[h, slot],
            send_sem=z_s.at[s, h, src], recv_sem=z_r.at[s, h, slot],
            device_id=line(zz, core), device_id_type=MESH,
        )

    def ag_copy(s, h, hact, d, block):
        return pltpu.make_async_remote_copy(
            src_ref=hact.at[h, block], dst_ref=hact.at[h, block],
            send_sem=ag_s.at[s, h, d - 1], recv_sem=ag_r.at[s, h, d - 1],
            device_id=line(xor(z, d), core), device_id_type=MESH,
        )

    def fw_copy(s, h, hact, zz, cc):
        return pltpu.make_async_remote_copy(
            src_ref=hact.at[h, cc * 4 + zz], dst_ref=hact.at[h, cc * 4 + zz],
            send_sem=fw_s.at[s, h, zz], recv_sem=fw_r.at[s, h, zz],
            device_id=line(z, 1 - core), device_id_type=MESH,
        )

    def rows_of(recv, h):
        return jnp.concatenate([recv[h, p].reshape(R, L) for p in range(NP)], axis=1)

    def contract(s, h, recv, product, part, sibr, zs, zr):
        def for_sibling(i, carry):
            part[h, i] = product(rows_of(recv, h), (1 - core) * 4 + 2 * i).astype(BF16)
            sib_copy(s, h, part, sibr, i).start()
            return carry

        lax.fori_loop(0, 2, for_sibling, 0)
        half = z // 2
        other = 1 - half
        far = product(rows_of(recv, h), core * 4 + 2 * other)
        sib_copy(s, h, part, sibr, other).wait_recv()
        far = far + sibr[h, other].astype(F32)
        zs[h, 0] = far[:, :Q].astype(BF16)
        zs[h, 1] = far[:, Q:].astype(BF16)
        low = lax.rem(z, 2)
        z_copy(s, h, zs, zr, low, xor(z, 2), 1).start()
        z_copy(s, h, zs, zr, 1 - low, xor(z, 3), 2).start()
        near = product(rows_of(recv, h), core * 4 + 2 * half)
        sib_copy(s, h, part, sibr, half).wait_recv()
        near = near + sibr[h, half].astype(F32)
        ownp[s, h, 0] = near[:, :Q]
        ownp[s, h, 1] = near[:, Q:]
        zs[h, 2] = ownp[s, h, 1 - low].astype(BF16)
        z_copy(s, h, zs, zr, 2, xor(z, 1), 0).start()

    def summed(s, h, zs, zr):
        low = lax.rem(z, 2)
        total = ownp[s, h, low]
        for d in range(1, 4):
            z_copy(s, h, zs, zr, 0, xor(z, d), d - 1).wait_recv()
            total = total + zr[h, d - 1].astype(F32)
        return total

    def spread(s, h, hact):
        for d in range(1, 4):
            ag_copy(s, h, hact, d, mine).start()
        fw_copy(s, h, hact, z, core).start()

    def forward(s, h, hact):
        for d in (1, 3, 2):
            zz = xor(z, d)
            ag_copy(s, h, hact, d, core * 4 + zz).wait_recv()
            fw_copy(s, h, hact, zz, core).start()

    def gather_wait(s, h, hact):
        for zz in range(4):
            fw_copy(s, h, hact, zz, 1 - core).wait_recv()

    def expand(k, h, hact, product, send, recv):
        def store(tile, group):
            for i in range(4):
                send[group * 4 + i, pl.ds(h * NB, NB)] = tile[:, i * L : (i + 1) * L].reshape(NB, CL, L)

        def row_of(group):
            rows = jnp.concatenate([hact[h, q] for q in range(8)], axis=1)
            store(product(rows, group).astype(BF16), group)

        def body(t, carry):
            group = lax.rem(y + 1 + t, 4)
            row_of(group)
            for i in range(4):
                p = group * 4 + lax.rem(xx + i, 4)
                a2a_copy(k, h, send, recv, p, me).start()
            return carry

        lax.fori_loop(0, 3, body, 0)
        row_of(y)
        for i in range(1, 4):
            a2a_copy(k, h, send, recv, y * 4 + lax.rem(xx + i, 4), me).start()

    def cols(w, block):
        return w[:, pl.ds(pl.multiple_of(block * Q, Q), 2 * Q)]

    def rows(w, block):
        return w[pl.ds(pl.multiple_of(block * Q, Q), 2 * Q), :]

    def norm_in(h):
        def body(i, carry):
            b = h * NB + i
            field = x_s[b].astype(F32)
            center = mean0(field)
            field = field - center
            scale = lax.rsqrt(mean0(field * field) + EPS)
            mu[b] = center
            rstd[b] = scale
            send1[:, b] = (field * scale * gin[...]).astype(BF16).reshape(NP, CL, L)
            return carry

        lax.fori_loop(0, NB, body, 0)

    def channel_part(h):
        def body(i, carry):
            l0, l1 = 2 * i, 2 * i + 1
            b0, b1 = h * NB + l0, h * NB + l1
            wide = jnp.concatenate([x_s[b0], x_s[b1]], axis=1).astype(F32)
            mixed = jnp.concatenate([recv2[h, :, l0].reshape(C, L), recv2[h, :, l1].reshape(C, L)], axis=1)
            first = wide + mixed.astype(F32)
            gain = jnp.concatenate([gmid[...], gmid[...]], axis=1)
            center = mean0(first)
            unit = first - center
            scale = lax.rsqrt(mean0(unit * unit) + EPS)
            unit = unit * scale
            normed = (unit * gain).astype(BF16)
            for kb in range(4):
                block = slice(kb * 256, kb * 256 + 256)
                value, slope = gelu_both(mm(cit[block, :], normed))
                inner_s[block, :] = value.astype(BF16)
                slope_s[block, :] = slope
            second = (first + mm(cot[...], inner_s[...])).astype(BF16)
            logits = mm(head16[...], second)[:8]
            target = jnp.concatenate([tgt[b0], tgt[b1]], axis=1)
            phases = lax.broadcasted_iota(jnp.int32, (8, 2 * L), 0).astype(F32)
            exps = jnp.exp(logits - jnp.max(logits, axis=0, keepdims=True))
            probs = exps / jnp.sum(exps, axis=0, keepdims=True)
            diff = probs - jnp.where(phases == target, 1.0, 0.0)
            slope16 = jnp.concatenate([diff, jnp.zeros((8, 2 * L), F32)], axis=0).astype(BF16)
            hp[...] += mm_nt(slope16, second)
            back_second = mm(headc[...], slope16)
            back_low = back_second.astype(BF16)
            for kb in range(4):
                block = slice(kb * 256, kb * 256 + 256)
                bip_s[block, :] = (mm(co[block, :], back_low) * slope_s[block, :]).astype(BF16)
            w = mm(ci[...], bip_s[...]) * gain
            back = back_second + scale * (w - mean0(w) - unit * mean0(w * unit))
            bf[b0] = back[:, :L]
            bf[b1] = back[:, L:]
            low = back.astype(BF16)
            send3[:, b0] = low[:, :L].reshape(NP, CL, L)
            send3[:, b1] = low[:, L:].reshape(NP, CL, L)
            return carry

        lax.fori_loop(0, NB // 2, body, 0)

    def norm_back(h):
        def body(i, carry):
            b = h * NB + i
            scale = rstd[b]
            unit = (x_s[b].astype(F32) - mu[b]) * scale
            w = recv4[h, :, i].reshape(C, L).astype(F32) * gin[...]
            bf[b] = bf[b] + scale * (w - mean0(w) - unit * mean0(w * unit))
            return carry

        lax.fori_loop(0, NB, body, 0)

    def out_copy(h):
        piece = pl.ds(h * NB, NB)
        return pltpu.make_async_copy(bf.at[piece], out_hbm.at[piece], out_sem.at[h])

    def ha_copy(i):
        return pltpu.make_async_remote_copy(
            src_ref=hsend.at[0], dst_ref=hbuf_a.at[ag], send_sem=ha_s.at[i], recv_sem=ha_r.at[i],
            device_id={"agent": lax.rem(ag + i, 8), "chan": chan, "batch": batch}, device_id_type=MESH,
        )

    def hy_copy(i):
        return pltpu.make_async_remote_copy(
            src_ref=hsend.at[1], dst_ref=hbuf_y.at[y], send_sem=hy_s.at[i], recv_sem=hy_r.at[i],
            device_id=plane(lax.rem(y + i, 4) * 4 + xx), device_id_type=MESH,
        )

    def hx_copy(i):
        return pltpu.make_async_remote_copy(
            src_ref=hsend.at[2], dst_ref=hbuf_x.at[xx], send_sem=hx_s.at[i], recv_sem=hx_r.at[i],
            device_id=plane(y * 4 + lax.rem(xx + i, 4)), device_id_type=MESH,
        )

    def total(buf, n):
        out = buf[0]
        for i in range(1, n):
            out = out + buf[i]
        return out

    loads[0].wait()
    norm_in(0)
    pl.semaphore_wait(barrier, NP - 1 + 7)
    a2a_send(0, 0, send1, recv1)
    for h in range(1, NC):
        norm_in(h)
        a2a_send(0, h, send1, recv1)
    loads[2].wait()
    loads[3].wait()
    for kb in range(4):
        block = slice(kb * 256, kb * 256 + 256)
        cit[block, :] = jnp.transpose(ci[:, block])
        cot[:, block] = jnp.transpose(co[block, :])
    loads[1].wait()
    for h in range(NC):
        a2a_wait(0, h, send1, recv1)
        contract(0, h, recv1, lambda a, block: mm(a, cols(win, block)), part1, sibr1, zs1, zr1)
    for h in range(NC):
        value, slope = gelu_both(summed(0, h, zs1, zr1))
        hact1[h, mine] = value.astype(BF16)
        hslope[h] = slope
        spread(0, h, hact1)
    loads[4].wait()
    for h in range(NC):
        forward(0, h, hact1)
        gather_wait(0, h, hact1)
        expand(1, h, hact1, lambda a, group: mm(a, cols(wout, group * 2)), send2, recv2)
    for h in range(NC):
        a2a_wait(1, h, send2, recv2)
        channel_part(h)
        a2a_send(2, h, send3, recv3)
    hsend[0] = hp[:8]
    hbuf_a[ag] = hp[:8]
    for i in range(1, 8):
        ha_copy(i).start()
    for h in range(NC):
        a2a_wait(2, h, send3, recv3)
        contract(1, h, recv3, lambda a, block: mm_nt(a, rows(wout, block)), part2, sibr2, zs2, zr2)
    for i in range(1, 8):
        ha_copy(i).wait()
    sums = total(hbuf_a, 8)
    hsend[1] = sums
    hbuf_y[y] = sums
    for i in range(1, 4):
        hy_copy(i).start()
    for h in range(NC):
        hact2[h, mine] = (summed(1, h, zs2, zr2) * hslope[h]).astype(BF16)
        spread(1, h, hact2)
    for i in range(1, 4):
        hy_copy(i).wait()
    sums = total(hbuf_y, 4)
    hsend[2] = sums
    hbuf_x[xx] = sums
    for i in range(1, 4):
        hx_copy(i).start()
    for h in range(NC):
        forward(1, h, hact2)
        gather_wait(1, h, hact2)
        expand(3, h, hact2, lambda a, group: mm_nt(a, rows(win, group * 2)), send4, recv4)
    for i in range(1, 4):
        hx_copy(i).wait()
    hg_ref[...] = total(hbuf_x, 4) * (1.0 / (B * A))
    for h in range(NC):
        a2a_wait(3, h, send4, recv4)
        norm_back(h)
        out_copy(h).start()

    for h in range(NC):
        for k, (send, recv) in enumerate(((send1, recv1), (send2, recv2), (send3, recv3), (send4, recv4))):
            a2a_drain(k, h, send, recv)
        for s, (part, sibr, zs, zr, hact) in enumerate(
            ((part1, sibr1, zs1, zr1, hact1), (part2, sibr2, zs2, zr2, hact2))
        ):
            for i in range(2):
                sib_copy(s, h, part, sibr, i).wait_send()
            for i in range(3):
                z_copy(s, h, zs, zr, i, xor(z, 1), 0).wait_send()
            for d in range(1, 4):
                ag_copy(s, h, hact, d, mine).wait_send()
            for zz in range(4):
                fw_copy(s, h, hact, zz, core).wait_send()
        out_copy(h).wait()


def fused(x, gin, win, wout, gmid, ci, co, head, actions, order):
    hbm = pl.BlockSpec(memory_space=pl.ANY)
    vmem = pl.BlockSpec(memory_space=pltpu.VMEM)
    dma = pltpu.SemaphoreType.DMA
    V = pltpu.VMEM
    exchange = V((NP, B, CL, L), BF16)
    arrive = V((NC, NP, NB, CL, L), BF16)
    scratch = [
        V((B, C, L), BF16), V((T, J), BF16), V((J, T), BF16),
        V((C, K), BF16), V((K, C), BF16), V((K, C), BF16), V((C, K), BF16),
        V((C, L), F32), V((C, L), F32), V((16, C), BF16), V((C, 16), BF16),
        V((B, 1, L), F32), V((B, 1, L), F32), V((B, 1, L), F32), V((B, C, L), F32),
        exchange, exchange, exchange, exchange, arrive, arrive, arrive, arrive,
        V((NC, 2, R, 2 * Q), BF16), V((NC, 2, R, 2 * Q), BF16),
        V((NC, 2, R, 2 * Q), BF16), V((NC, 2, R, 2 * Q), BF16),
        V((NC, 3, R, Q), BF16), V((NC, 3, R, Q), BF16),
        V((NC, 3, R, Q), BF16), V((NC, 3, R, Q), BF16),
        V((NC, 8, R, Q), BF16), V((NC, 8, R, Q), BF16),
        V((2, NC, 2, R, Q), F32), V((NC, R, Q), F32),
        V((K, 2 * L), BF16), V((K, 2 * L), F32), V((K, 2 * L), BF16), V((16, C), F32),
        V((8, 8, C), F32), V((4, 8, C), F32), V((4, 8, C), F32), V((3, 8, C), F32),
        dma((5,)), dma((NC,)), dma((4, NC, NP)), dma((4, NC, NP)),
        dma((2, NC, 2)), dma((2, NC, 2)), dma((2, NC, 3)), dma((2, NC, 3)),
        dma((2, NC, 3)), dma((2, NC, 3)), dma((2, NC, 4)), dma((2, NC, 4)),
        dma((8,)), dma((8,)), dma((4,)), dma((4,)), dma((4,)), dma((4,)),
    ]
    return pl.pallas_call(
        kernel,
        out_shape=(jax.ShapeDtypeStruct((B, C, L), F32), jax.ShapeDtypeStruct((8, C), F32)),
        in_specs=[hbm, vmem, hbm, hbm, vmem, hbm, hbm, vmem, vmem, vmem],
        out_specs=(hbm, vmem),
        scratch_shapes=scratch,
        compiler_params=pltpu.CompilerParams(
            collective_id=0, has_side_effects=True, vmem_limit_bytes=58 << 20
        ),
    )(x, gin, win, wout, gmid, ci, co, head, actions, order)


def shards(features, norm_gain, tok_in, tok_out, mix_gain, chan_in, chan_out, head, actions, order):
    grad, head_grad = fused(
        jnp.transpose(features, (1, 0, 2)),
        norm_gain.reshape(1, C),
        tok_in,
        tok_out,
        mix_gain.reshape(1, C),
        chan_in,
        chan_out,
        head.T,
        actions,
        order.reshape(1, L),
    )
    return jnp.transpose(grad, (1, 0, 2)), head_grad.T


def solution(mesh):
    in_specs = (
        P(None, None, ("agent", "chan", "batch")),
        P(),
        P("agent", None),
        P(None, "agent"),
        P(),
        P(),
        P(),
        P(),
        P(None, ("agent", "chan", "batch")),
        P(("agent", "chan", "batch")),
    )
    out_specs = (P(None, None, ("agent", "chan", "batch")), P())
    return jax.shard_map(shards, mesh=mesh, in_specs=in_specs, out_specs=out_specs, check_vma=False)
```

```python
import jax
import jax.numpy as jnp
from jax import lax
from jax.experimental import pallas as pl
from jax.experimental.pallas import tpu as pltpu
from jax.sharding import PartitionSpec as P

MESH = pl.DeviceIdType.MESH
F32 = jnp.float32
BF16 = jnp.bfloat16

A = 16384
B = 16
C = 256
L = 128
NP = 16
CL = C // NP
T = NP * L
J = 2048
K = 1024
NC = 2
NB = B // NC
R = NB * CL
G = 8
KB = 256
Q = J // 8

GELU_K = 0.7978845608028654
GELU_C = 0.044715
EPS = 1e-05


def mm(a, b):
    return lax.dot_general(a, b, (((1,), (0,)), ((), ())), preferred_element_type=F32)


def mm_nt(a, b):
    return lax.dot_general(a, b, (((1,), (1,)), ((), ())), preferred_element_type=F32)


def gelu_both(v):
    square = v * v
    half = 0.5 + 0.5 * jnp.tanh(v * (GELU_K + (GELU_K * GELU_C) * square))
    value = v * half
    slope = half + value * (1.0 - half) * (2.0 * GELU_K + (6.0 * GELU_K * GELU_C) * square)
    return value, slope


def mean0(v):
    return jnp.sum(v, axis=0, keepdims=True) * (1.0 / C)


def kernel(
    x_hbm, gin_ref, win_hbm, wout_hbm, gmid_ref, ci_hbm, co_hbm, head_ref, act_ref, ord_ref,
    out_hbm, hg_ref,
    x_raw, x_s, win, wout, ci, co, cit, cot, gin, gmid, head16, headc, tgt, mu, rstd, bf,
    send1, send2, send3, send4, recv1, recv2, recv3, recv4,
    part1, part2, sibr1, sibr2, zs1, zs2, zr1, zr2, hact1, hact2, ownp, hslope,
    inner_s, slope_s, bip_s, hp, hbuf_a, hbuf_y, hbuf_x, hsend,
    ld_sem, out_sem, a2a_s, a2a_r, sib_s, sib_r, z_s, z_r, ag_s, ag_r, fw_s, fw_r,
    ha_s, ha_r, hy_s, hy_r, hx_s, hx_r,
):
    ag = lax.axis_index("agent")
    chan = lax.axis_index("chan")
    batch = lax.axis_index("batch")
    me = chan * 2 + batch
    z = ag // 2
    core = lax.rem(ag, 2)
    y = me // 4
    xx = lax.rem(me, 4)
    mine = core * 4 + z

    def plane(p):
        return {"agent": ag, "chan": p // 2, "batch": lax.rem(p, 2)}

    def line(zz, cc):
        return {"agent": zz * 2 + cc, "chan": chan, "batch": batch}

    def xor(a, d):
        out = a
        if d & 1:
            out = out + 1 - 2 * lax.rem(out, 2)
        if d & 2:
            out = lax.rem(out + 2, 4)
        return out

    loads = [
        pltpu.make_async_copy(x_hbm, x_raw, ld_sem.at[0]),
        pltpu.make_async_copy(win_hbm, win, ld_sem.at[1]),
        pltpu.make_async_copy(ci_hbm, ci, ld_sem.at[2]),
        pltpu.make_async_copy(co_hbm, co, ld_sem.at[3]),
        pltpu.make_async_copy(wout_hbm, wout, ld_sem.at[4]),
    ]
    loads[0].start()

    barrier = pltpu.get_barrier_semaphore()
    for i in range(1, NP):
        pl.semaphore_signal(barrier, inc=1, device_id=plane(lax.rem(me + i, NP)), device_id_type=MESH)
    for i in range(1, 8):
        pl.semaphore_signal(
            barrier, inc=1,
            device_id={"agent": lax.rem(ag + i, 8), "chan": chan, "batch": batch},
            device_id_type=MESH,
        )

    gin[...] = jnp.transpose(jnp.broadcast_to(gin_ref[...], (L, C)))

    def a2a_copy(k, h, send, recv, p, slot):
        return pltpu.make_async_remote_copy(
            src_ref=send.at[p, pl.ds(h * NB, NB)],
            dst_ref=recv.at[h, slot],
            send_sem=a2a_s.at[k, h],
            recv_sem=a2a_r.at[k, h],
            device_id=plane(p),
            device_id_type=MESH,
        )

    def a2a_send(k, h, send, recv):
        def body(i, carry):
            a2a_copy(k, h, send, recv, lax.rem(me + i, NP), me).start()
            return carry

        lax.fori_loop(1, NP, body, 0)

    def a2a_wait(k, h, send, recv):
        recv[h, me] = send[me, pl.ds(h * NB, NB)]
        others = recv.at[h, pl.ds(0, NP - 1)]
        pltpu.make_async_copy(others, others, a2a_r.at[k, h]).wait()

    def a2a_drain(k, h, send, recv):
        others = recv.at[h, pl.ds(0, NP - 1)]
        pltpu.make_async_copy(others, others, a2a_s.at[k, h]).wait()

    def sib_copy(s, h, part, sibr, i):
        return pltpu.make_async_remote_copy(
            src_ref=part.at[h, i], dst_ref=sibr.at[h, i],
            send_sem=sib_s.at[s, h, i], recv_sem=sib_r.at[s, h, i],
            device_id=line(z, 1 - core), device_id_type=MESH,
        )

    def z_copy(s, h, zs, zr, src, zz, slot):
        return pltpu.make_async_remote_copy(
            src_ref=zs.at[h, src], dst_ref=zr.at[h, slot],
            send_sem=z_s.at[s, h, src], recv_sem=z_r.at[s, h, slot],
            device_id=line(zz, core), device_id_type=MESH,
        )

    def ag_copy(s, h, hact, d, block):
        return pltpu.make_async_remote_copy(
            src_ref=hact.at[h, block], dst_ref=hact.at[h, block],
            send_sem=ag_s.at[s, h, d - 1], recv_sem=ag_r.at[s, h, d - 1],
            device_id=line(xor(z, d), core), device_id_type=MESH,
        )

    def fw_copy(s, h, hact, zz, cc):
        return pltpu.make_async_remote_copy(
            src_ref=hact.at[h, cc * 4 + zz], dst_ref=hact.at[h, cc * 4 + zz],
            send_sem=fw_s.at[s, h, zz], recv_sem=fw_r.at[s, h, zz],
            device_id=line(z, 1 - core), device_id_type=MESH,
        )

    def rows_of(recv, h):
        return jnp.concatenate([recv[h, p].reshape(R, L) for p in range(NP)], axis=1)

    def contract(s, h, recv, product, part, sibr, zs, zr):
        def for_sibling(i, carry):
            part[h, i] = product(rows_of(recv, h), (1 - core) * 4 + 2 * i).astype(BF16)
            sib_copy(s, h, part, sibr, i).start()
            return carry

        lax.fori_loop(0, 2, for_sibling, 0)
        half = z // 2
        other = 1 - half
        far = product(rows_of(recv, h), core * 4 + 2 * other)
        sib_copy(s, h, part, sibr, other).wait_recv()
        far = far + sibr[h, other].astype(F32)
        zs[h, 0] = far[:, :Q].astype(BF16)
        zs[h, 1] = far[:, Q:].astype(BF16)
        low = lax.rem(z, 2)
        z_copy(s, h, zs, zr, low, xor(z, 2), 1).start()
        z_copy(s, h, zs, zr, 1 - low, xor(z, 3), 2).start()
        near = product(rows_of(recv, h), core * 4 + 2 * half)
        sib_copy(s, h, part, sibr, half).wait_recv()
        near = near + sibr[h, half].astype(F32)
        ownp[s, h, 0] = near[:, :Q]
        ownp[s, h, 1] = near[:, Q:]
        zs[h, 2] = ownp[s, h, 1 - low].astype(BF16)
        z_copy(s, h, zs, zr, 2, xor(z, 1), 0).start()

    def summed(s, h, zs, zr):
        low = lax.rem(z, 2)
        total = ownp[s, h, low]
        for d in range(1, 4):
            z_copy(s, h, zs, zr, 0, xor(z, d), d - 1).wait_recv()
            total = total + zr[h, d - 1].astype(F32)
        return total

    def spread(s, h, hact):
        for d in range(1, 4):
            ag_copy(s, h, hact, d, mine).start()
        fw_copy(s, h, hact, z, core).start()

    def forward(s, h, hact):
        for d in (1, 3, 2):
            zz = xor(z, d)
            ag_copy(s, h, hact, d, core * 4 + zz).wait_recv()
            fw_copy(s, h, hact, zz, core).start()

    def gather_wait(s, h, hact):
        for zz in range(4):
            fw_copy(s, h, hact, zz, 1 - core).wait_recv()

    def expand(k, h, hact, product, send, recv):
        def store(tile, group):
            for i in range(4):
                send[group * 4 + i, pl.ds(h * NB, NB)] = tile[:, i * L : (i + 1) * L].reshape(NB, CL, L)

        def row_of(group):
            rows = jnp.concatenate([hact[h, q] for q in range(8)], axis=1)
            store(product(rows, group).astype(BF16), group)

        def body(t, carry):
            group = lax.rem(y + 1 + t, 4)
            row_of(group)
            for i in range(4):
                p = group * 4 + lax.rem(xx + i, 4)
                a2a_copy(k, h, send, recv, p, me).start()
            return carry

        lax.fori_loop(0, 3, body, 0)
        row_of(y)
        for i in range(1, 4):
            a2a_copy(k, h, send, recv, y * 4 + lax.rem(xx + i, 4), me).start()

    def cols(w, block):
        return w[:, pl.ds(pl.multiple_of(block * Q, Q), 2 * Q)]

    def rows(w, block):
        return w[pl.ds(pl.multiple_of(block * Q, Q), 2 * Q), :]

    def norm_in(h):
        def body(i, carry):
            b = h * NB + i
            field = x_s[b].astype(F32)
            center = mean0(field)
            field = field - center
            scale = lax.rsqrt(mean0(field * field) + EPS)
            mu[b] = center
            rstd[b] = scale
            send1[:, b] = (field * scale * gin[...]).astype(BF16).reshape(NP, CL, L)
            return carry

        lax.fori_loop(0, NB, body, 0)

    def channel_part(h):
        def body(i, carry):
            local = [G * i + g for g in range(G)]
            at = [h * NB + b for b in local]

            def lanes(pieces):
                return jnp.concatenate(pieces, axis=1)

            wide = lanes([x_s[b] for b in at]).astype(F32)
            mixed = lanes([recv2[h, :, b].reshape(C, L) for b in local])
            first = wide + mixed.astype(F32)
            gain = lanes([gmid[...]] * G)
            center = mean0(first)
            unit = first - center
            scale = lax.rsqrt(mean0(unit * unit) + EPS)
            unit = unit * scale
            normed = (unit * gain).astype(BF16)
            for kb in range(K // KB):
                block = slice(kb * KB, kb * KB + KB)
                value, slope = gelu_both(mm(cit[block, :], normed))
                inner_s[block, :] = value.astype(BF16)
                slope_s[block, :] = slope
            second = (first + mm(cot[...], inner_s[...])).astype(BF16)
            logits = mm(head16[...], second)[:8]
            target = lanes([tgt[b] for b in at])
            phases = lax.broadcasted_iota(jnp.int32, (8, G * L), 0).astype(F32)
            exps = jnp.exp(logits - jnp.max(logits, axis=0, keepdims=True))
            probs = exps / jnp.sum(exps, axis=0, keepdims=True)
            diff = probs - jnp.where(phases == target, 1.0, 0.0)
            slope16 = jnp.concatenate([diff, jnp.zeros((8, G * L), F32)], axis=0).astype(BF16)
            hp[...] += mm_nt(slope16, second)
            back_second = mm(headc[...], slope16)
            back_low = back_second.astype(BF16)
            for kb in range(K // KB):
                block = slice(kb * KB, kb * KB + KB)
                bip_s[block, :] = (mm(co[block, :], back_low) * slope_s[block, :]).astype(BF16)
            w = mm(ci[...], bip_s[...]) * gain
            back = back_second + scale * (w - mean0(w) - unit * mean0(w * unit))
            low = back.astype(BF16)
            for g in range(G):
                bf[at[g]] = back[:, g * L : (g + 1) * L]
                send3[:, at[g]] = low[:, g * L : (g + 1) * L].reshape(NP, CL, L)
            return carry

        lax.fori_loop(0, NB // G, body, 0)

    def norm_back(h):
        def body(i, carry):
            b = h * NB + i
            scale = rstd[b]
            unit = (x_s[b].astype(F32) - mu[b]) * scale
            w = recv4[h, :, i].reshape(C, L).astype(F32) * gin[...]
            bf[b] = bf[b] + scale * (w - mean0(w) - unit * mean0(w * unit))
            out_copy(b).start()
            return carry

        lax.fori_loop(0, NB, body, 0)

    def out_copy(b):
        return pltpu.make_async_copy(bf.at[b], out_hbm.at[:, b], out_sem.at[b])

    def line_drain(s, h, part, sibr, zs, zr, hact):
        for i in range(2):
            sib_copy(s, h, part, sibr, i).wait_send()
        for i in range(3):
            z_copy(s, h, zs, zr, i, xor(z, 1), 0).wait_send()
        for d in range(1, 4):
            ag_copy(s, h, hact, d, mine).wait_send()
        for zz in range(4):
            fw_copy(s, h, hact, zz, core).wait_send()

    def ha_copy(i):
        return pltpu.make_async_remote_copy(
            src_ref=hsend.at[0], dst_ref=hbuf_a.at[ag], send_sem=ha_s.at[i], recv_sem=ha_r.at[i],
            device_id={"agent": lax.rem(ag + i, 8), "chan": chan, "batch": batch}, device_id_type=MESH,
        )

    def hy_copy(i):
        return pltpu.make_async_remote_copy(
            src_ref=hsend.at[1], dst_ref=hbuf_y.at[y], send_sem=hy_s.at[i], recv_sem=hy_r.at[i],
            device_id=plane(lax.rem(y + i, 4) * 4 + xx), device_id_type=MESH,
        )

    def hx_copy(i):
        return pltpu.make_async_remote_copy(
            src_ref=hsend.at[2], dst_ref=hbuf_x.at[xx], send_sem=hx_s.at[i], recv_sem=hx_r.at[i],
            device_id=plane(y * 4 + lax.rem(xx + i, 4)), device_id_type=MESH,
        )

    def total(buf, n):
        out = buf[0]
        for i in range(1, n):
            out = out + buf[i]
        return out

    loads[0].wait()

    def samples_first(h):
        def body(i, carry):
            piece = pl.ds(pl.multiple_of(i * CL, CL), CL)
            field = x_raw[piece].astype(F32)[:, h * NB : (h + 1) * NB]
            x_s[h * NB : (h + 1) * NB, piece] = jnp.transpose(field, (1, 0, 2)).astype(BF16)
            return carry

        lax.fori_loop(0, NP, body, 0)

    samples_first(0)
    norm_in(0)
    pl.semaphore_wait(barrier, NP - 1 + 7)
    a2a_send(0, 0, send1, recv1)
    for load in loads[1:]:
        load.start()
    for h in range(1, NC):
        samples_first(h)
        norm_in(h)
        a2a_drain(0, h - 1, send1, recv1)
        a2a_send(0, h, send1, recv1)
    gmid[...] = jnp.transpose(jnp.broadcast_to(gmid_ref[...], (L, C)))
    head_rows = jnp.concatenate([head_ref[...].astype(F32), jnp.zeros((8, C), F32)], axis=0)
    head16[...] = head_rows.astype(BF16)
    wide_head = jnp.concatenate([head_rows, jnp.zeros((L - 16, C), F32)], axis=0)
    headc[...] = jnp.transpose(wide_head)[:, :16].astype(BF16)
    spot = lax.broadcasted_iota(jnp.int32, (L, L), 0) == lax.rem(ord_ref[...], L)
    targets = mm(act_ref[...].astype(F32).astype(BF16), spot.astype(F32).astype(BF16))
    for b in range(B):
        tgt[b] = targets[b : b + 1, :]
    hp[...] = jnp.zeros((16, C), F32)

    loads[2].wait()
    loads[3].wait()
    for kb in range(4):
        block = slice(kb * 256, kb * 256 + 256)
        cit[block, :] = jnp.transpose(ci[:, block])
        cot[:, block] = jnp.transpose(co[block, :])
    loads[1].wait()
    for h in range(NC):
        a2a_wait(0, h, send1, recv1)
        contract(0, h, recv1, lambda a, block: mm(a, cols(win, block)), part1, sibr1, zs1, zr1)
    for h in range(NC):
        value, slope = gelu_both(summed(0, h, zs1, zr1))
        hact1[h, mine] = value.astype(BF16)
        hslope[h] = slope
        spread(0, h, hact1)
    loads[4].wait()
    for h in range(NC):
        forward(0, h, hact1)
        gather_wait(0, h, hact1)
        expand(1, h, hact1, lambda a, group: mm(a, cols(wout, group * 2)), send2, recv2)
    for h in range(NC):
        a2a_wait(1, h, send2, recv2)
        channel_part(h)
        a2a_send(2, h, send3, recv3)
    a2a_drain(0, NC - 1, send1, recv1)
    for h in range(NC):
        line_drain(0, h, part1, sibr1, zs1, zr1, hact1)
        a2a_drain(1, h, send2, recv2)
    hsend[0] = hp[:8]
    hbuf_a[ag] = hp[:8]
    for i in range(1, 8):
        ha_copy(i).start()
    for h in range(NC):
        a2a_wait(2, h, send3, recv3)
        contract(1, h, recv3, lambda a, block: mm_nt(a, rows(wout, block)), part2, sibr2, zs2, zr2)
    for i in range(1, 8):
        ha_copy(i).wait()
    sums = total(hbuf_a, 8)
    hsend[1] = sums
    hbuf_y[y] = sums
    for i in range(1, 4):
        hy_copy(i).start()
    for h in range(NC):
        hact2[h, mine] = (summed(1, h, zs2, zr2) * hslope[h]).astype(BF16)
        spread(1, h, hact2)
    for i in range(1, 4):
        hy_copy(i).wait()
    sums = total(hbuf_y, 4)
    hsend[2] = sums
    hbuf_x[xx] = sums
    for i in range(1, 4):
        hx_copy(i).start()
    for h in range(NC):
        forward(1, h, hact2)
        gather_wait(1, h, hact2)
        expand(3, h, hact2, lambda a, group: mm_nt(a, rows(win, group * 2)), send4, recv4)
    for i in range(1, 4):
        hx_copy(i).wait()
    hg_ref[...] = total(hbuf_x, 4) * (1.0 / (B * A))
    for h in range(NC):
        a2a_drain(2, h, send3, recv3)
        line_drain(1, h, part2, sibr2, zs2, zr2, hact2)
        if h < NC - 1:
            a2a_drain(3, h, send4, recv4)
    for h in range(NC):
        a2a_wait(3, h, send4, recv4)
        norm_back(h)

    a2a_drain(3, NC - 1, send4, recv4)
    for b in range(B):
        out_copy(b).wait()


def fused(x, gin, win, wout, gmid, ci, co, head, actions, order):
    hbm = pl.BlockSpec(memory_space=pl.ANY)
    vmem = pl.BlockSpec(memory_space=pltpu.VMEM)
    dma = pltpu.SemaphoreType.DMA
    V = pltpu.VMEM
    exchange = V((NP, B, CL, L), BF16)
    arrive = V((NC, NP, NB, CL, L), BF16)
    scratch = [
        V((C, B, L), BF16), V((B, C, L), BF16), V((T, J), BF16), V((J, T), BF16),
        V((C, K), BF16), V((K, C), BF16), V((K, C), BF16), V((C, K), BF16),
        V((C, L), F32), V((C, L), F32), V((16, C), BF16), V((C, 16), BF16),
        V((B, 1, L), F32), V((B, 1, L), F32), V((B, 1, L), F32), V((B, C, L), F32),
        exchange, exchange, exchange, exchange, arrive, arrive, arrive, arrive,
        V((NC, 2, R, 2 * Q), BF16), V((NC, 2, R, 2 * Q), BF16),
        V((NC, 2, R, 2 * Q), BF16), V((NC, 2, R, 2 * Q), BF16),
        V((NC, 3, R, Q), BF16), V((NC, 3, R, Q), BF16),
        V((NC, 3, R, Q), BF16), V((NC, 3, R, Q), BF16),
        V((NC, 8, R, Q), BF16), V((NC, 8, R, Q), BF16),
        V((2, NC, 2, R, Q), F32), V((NC, R, Q), F32),
        V((K, G * L), BF16), V((K, G * L), F32), V((K, G * L), BF16), V((16, C), F32),
        V((8, 8, C), F32), V((4, 8, C), F32), V((4, 8, C), F32), V((3, 8, C), F32),
        dma((5,)), dma((B,)), dma((4, NC)), dma((4, NC)),
        dma((2, NC, 2)), dma((2, NC, 2)), dma((2, NC, 3)), dma((2, NC, 3)),
        dma((2, NC, 3)), dma((2, NC, 3)), dma((2, NC, 4)), dma((2, NC, 4)),
        dma((8,)), dma((8,)), dma((4,)), dma((4,)), dma((4,)), dma((4,)),
    ]
    return pl.pallas_call(
        kernel,
        out_shape=(jax.ShapeDtypeStruct((C, B, L), F32), jax.ShapeDtypeStruct((8, C), F32)),
        in_specs=[hbm, vmem, hbm, hbm, vmem, hbm, hbm, vmem, vmem, vmem],
        out_specs=(hbm, vmem),
        scratch_shapes=scratch,
        compiler_params=pltpu.CompilerParams(
            collective_id=0, has_side_effects=True, vmem_limit_bytes=58 << 20
        ),
    )(x, gin, win, wout, gmid, ci, co, head, actions, order)


def shards(features, norm_gain, tok_in, tok_out, mix_gain, chan_in, chan_out, head, actions, order):
    grad, head_grad = fused(
        features,
        norm_gain.reshape(1, C),
        tok_in,
        tok_out,
        mix_gain.reshape(1, C),
        chan_in,
        chan_out,
        head.T,
        actions,
        order.reshape(1, L),
    )
    return grad, head_grad.T


def solution(mesh):
    in_specs = (
        P(None, None, ("agent", "chan", "batch")),
        P(),
        P("agent", None),
        P(None, "agent"),
        P(),
        P(),
        P(),
        P(),
        P(None, ("agent", "chan", "batch")),
        P(("agent", "chan", "batch")),
    )
    out_specs = (P(None, None, ("agent", "chan", "batch")), P())
    return jax.shard_map(shards, mesh=mesh, in_specs=in_specs, out_specs=out_specs, check_vma=False)
```

```python
import jax
import jax.numpy as jnp
from jax import lax
from jax.experimental import pallas as pl
from jax.experimental.pallas import tpu as pltpu
from jax.sharding import PartitionSpec as P

MESH = pl.DeviceIdType.MESH
F32 = jnp.float32
BF16 = jnp.bfloat16

A = 16384
B = 16
C = 256
L = 128
NP = 16
CL = C // NP
T = NP * L
J = 2048
K = 1024
NC = 2
NB = B // NC
R = NB * CL
G = 4
KB = 256
PIECES = 8
Q = J // 8

GELU_K = 0.7978845608028654
GELU_C = 0.044715
EPS = 1e-05


def mm(a, b):
    return lax.dot_general(a, b, (((1,), (0,)), ((), ())), preferred_element_type=F32)


def mm_nt(a, b):
    return lax.dot_general(a, b, (((1,), (1,)), ((), ())), preferred_element_type=F32)


def gelu_both(v):
    square = v * v
    half = 0.5 + 0.5 * jnp.tanh(v * (GELU_K + (GELU_K * GELU_C) * square))
    value = v * half
    slope = half + value * (1.0 - half) * (2.0 * GELU_K + (6.0 * GELU_K * GELU_C) * square)
    return value, slope


def mean0(v):
    return jnp.sum(v, axis=0, keepdims=True) * (1.0 / C)


def kernel(
    x_hbm, gin_ref, win_hbm, wout_hbm, gmid_ref, ci_hbm, co_hbm, head_ref, act_ref, ord_ref,
    out_hbm, hg_ref,
    x_raw, x_s, win, wout, ci, co, cit, cot, gin, gmid, head16, headc, tgt, mu, rstd, bf,
    send1, send2, send3, send4, recv1, recv2, recv3, recv4,
    part1, part2, sibr1, sibr2, zs1, zs2, zr1, zr2, hact1, hact2, ownp, hslope,
    inner_s, slope_s, bip_s, hp, hbuf_a, hbuf_y, hbuf_x, hsend,
    ld_sem, out_sem, a2a_s, a2a_r, sib_s, sib_r, z_s, z_r, ag_s, ag_r, fw_s, fw_r,
    ha_s, ha_r, hy_s, hy_r, hx_s, hx_r,
):
    ag = lax.axis_index("agent")
    chan = lax.axis_index("chan")
    batch = lax.axis_index("batch")
    me = chan * 2 + batch
    z = ag // 2
    core = lax.rem(ag, 2)
    y = me // 4
    xx = lax.rem(me, 4)
    mine = core * 4 + z

    def plane(p):
        return {"agent": ag, "chan": p // 2, "batch": lax.rem(p, 2)}

    def line(zz, cc):
        return {"agent": zz * 2 + cc, "chan": chan, "batch": batch}

    def xor(a, d):
        out = a
        if d & 1:
            out = out + 1 - 2 * lax.rem(out, 2)
        if d & 2:
            out = lax.rem(out + 2, 4)
        return out

    loads = [
        pltpu.make_async_copy(x_hbm, x_raw, ld_sem.at[0]),
        pltpu.make_async_copy(win_hbm, win, ld_sem.at[1]),
        pltpu.make_async_copy(ci_hbm, ci, ld_sem.at[2]),
        pltpu.make_async_copy(co_hbm, co, ld_sem.at[3]),
        pltpu.make_async_copy(wout_hbm, wout, ld_sem.at[4]),
    ]
    loads[0].start()

    barrier = pltpu.get_barrier_semaphore()
    for i in range(1, NP):
        pl.semaphore_signal(barrier, inc=1, device_id=plane(lax.rem(me + i, NP)), device_id_type=MESH)
    for i in range(1, 8):
        pl.semaphore_signal(
            barrier, inc=1,
            device_id={"agent": lax.rem(ag + i, 8), "chan": chan, "batch": batch},
            device_id_type=MESH,
        )

    gin[...] = jnp.transpose(jnp.broadcast_to(gin_ref[...], (L, C)))

    def a2a_copy(k, h, send, recv, p, slot):
        return pltpu.make_async_remote_copy(
            src_ref=send.at[p, pl.ds(h * NB, NB)],
            dst_ref=recv.at[h, slot],
            send_sem=a2a_s.at[k, h],
            recv_sem=a2a_r.at[k, h],
            device_id=plane(p),
            device_id_type=MESH,
        )

    def a2a_send(k, h, send, recv):
        def body(i, carry):
            a2a_copy(k, h, send, recv, lax.rem(me + i, NP), me).start()
            return carry

        lax.fori_loop(1, NP, body, 0)

    def send_step(k, h, i, send, recv):
        def body(d, carry):
            p = lax.rem(me + d, NP)
            pltpu.make_async_remote_copy(
                src_ref=send.at[p, pl.ds(h * NB + i * G, G)],
                dst_ref=recv.at[h, me, pl.ds(i * G, G)],
                send_sem=a2a_s.at[k, h],
                recv_sem=a2a_r.at[k, h],
                device_id=plane(p),
                device_id_type=MESH,
            ).start()
            return carry

        lax.fori_loop(1, NP, body, 0)

    def a2a_wait(k, h, send, recv):
        recv[h, me] = send[me, pl.ds(h * NB, NB)]
        others = recv.at[h, pl.ds(0, NP - 1)]
        pltpu.make_async_copy(others, others, a2a_r.at[k, h]).wait()

    def a2a_drain(k, h, send, recv):
        others = recv.at[h, pl.ds(0, NP - 1)]
        pltpu.make_async_copy(others, others, a2a_s.at[k, h]).wait()

    def sib_copy(s, h, part, sibr, i):
        return pltpu.make_async_remote_copy(
            src_ref=part.at[h, i], dst_ref=sibr.at[h, i],
            send_sem=sib_s.at[s, h, i], recv_sem=sib_r.at[s, h, i],
            device_id=line(z, 1 - core), device_id_type=MESH,
        )

    def z_copy(s, h, zs, zr, src, zz, slot):
        return pltpu.make_async_remote_copy(
            src_ref=zs.at[h, src], dst_ref=zr.at[h, slot],
            send_sem=z_s.at[s, h, src], recv_sem=z_r.at[s, h, slot],
            device_id=line(zz, core), device_id_type=MESH,
        )

    def ag_copy(s, h, hact, d, block):
        return pltpu.make_async_remote_copy(
            src_ref=hact.at[h, block], dst_ref=hact.at[h, block],
            send_sem=ag_s.at[s, h, d - 1], recv_sem=ag_r.at[s, h, d - 1],
            device_id=line(xor(z, d), core), device_id_type=MESH,
        )

    def fw_copy(s, h, hact, zz, cc):
        return pltpu.make_async_remote_copy(
            src_ref=hact.at[h, cc * 4 + zz], dst_ref=hact.at[h, cc * 4 + zz],
            send_sem=fw_s.at[s, h, zz], recv_sem=fw_r.at[s, h, zz],
            device_id=line(z, 1 - core), device_id_type=MESH,
        )

    def rows_of(recv, h):
        return jnp.concatenate([recv[h, p].reshape(R, L) for p in range(NP)], axis=1)

    def contract(s, h, recv, product, part, sibr, zs, zr):
        def for_sibling(i, carry):
            part[h, i] = product(rows_of(recv, h), (1 - core) * 4 + 2 * i).astype(BF16)
            sib_copy(s, h, part, sibr, i).start()
            return carry

        lax.fori_loop(0, 2, for_sibling, 0)
        half = z // 2
        other = 1 - half
        far = product(rows_of(recv, h), core * 4 + 2 * other)
        sib_copy(s, h, part, sibr, other).wait_recv()
        far = far + sibr[h, other].astype(F32)
        zs[h, 0] = far[:, :Q].astype(BF16)
        zs[h, 1] = far[:, Q:].astype(BF16)
        low = lax.rem(z, 2)
        z_copy(s, h, zs, zr, low, xor(z, 2), 1).start()
        z_copy(s, h, zs, zr, 1 - low, xor(z, 3), 2).start()
        near = product(rows_of(recv, h), core * 4 + 2 * half)
        sib_copy(s, h, part, sibr, half).wait_recv()
        near = near + sibr[h, half].astype(F32)
        ownp[s, h, 0] = near[:, :Q]
        ownp[s, h, 1] = near[:, Q:]
        zs[h, 2] = ownp[s, h, 1 - low].astype(BF16)
        z_copy(s, h, zs, zr, 2, xor(z, 1), 0).start()

    def summed(s, h, zs, zr):
        low = lax.rem(z, 2)
        total = ownp[s, h, low]
        for d in range(1, 4):
            z_copy(s, h, zs, zr, 0, xor(z, d), d - 1).wait_recv()
            total = total + zr[h, d - 1].astype(F32)
        return total

    def spread(s, h, hact):
        for d in range(1, 4):
            ag_copy(s, h, hact, d, mine).start()
        fw_copy(s, h, hact, z, core).start()

    def forward(s, h, hact):
        for d in (1, 3, 2):
            zz = xor(z, d)
            ag_copy(s, h, hact, d, core * 4 + zz).wait_recv()
            fw_copy(s, h, hact, zz, core).start()

    def gather_wait(s, h, hact):
        for zz in range(4):
            fw_copy(s, h, hact, zz, 1 - core).wait_recv()

    def expand(k, h, hact, product, send, recv):
        def store(tile, group):
            for i in range(4):
                send[group * 4 + i, pl.ds(h * NB, NB)] = tile[:, i * L : (i + 1) * L].reshape(NB, CL, L)

        def row_of(group):
            rows = jnp.concatenate([hact[h, q] for q in range(8)], axis=1)
            store(product(rows, group).astype(BF16), group)

        def body(t, carry):
            group = lax.rem(y + 1 + t, 4)
            row_of(group)
            for i in range(4):
                p = group * 4 + lax.rem(xx + i, 4)
                a2a_copy(k, h, send, recv, p, me).start()
            return carry

        lax.fori_loop(0, 3, body, 0)
        row_of(y)
        for i in range(1, 4):
            a2a_copy(k, h, send, recv, y * 4 + lax.rem(xx + i, 4), me).start()

    def cols(w, block):
        return w[:, pl.ds(pl.multiple_of(block * Q, Q), 2 * Q)]

    def rows(w, block):
        return w[pl.ds(pl.multiple_of(block * Q, Q), 2 * Q), :]

    def norm_in(first, count):
        def body(i, carry):
            b = first + i
            field = x_s[b].astype(F32)
            center = mean0(field)
            field = field - center
            scale = lax.rsqrt(mean0(field * field) + EPS)
            mu[b] = center
            rstd[b] = scale
            send1[:, b] = (field * scale * gin[...]).astype(BF16).reshape(NP, CL, L)
            return carry

        lax.fori_loop(0, count, body, 0)

    def channel_part(h):
        def body(i, carry):
            local = [G * i + g for g in range(G)]
            at = [h * NB + b for b in local]

            def lanes(pieces):
                return jnp.concatenate(pieces, axis=1)

            wide = lanes([x_s[b] for b in at]).astype(F32)
            mixed = lanes([recv2[h, :, b].reshape(C, L) for b in local])
            first = wide + mixed.astype(F32)
            gain = lanes([gmid[...]] * G)
            center = mean0(first)
            unit = first - center
            scale = lax.rsqrt(mean0(unit * unit) + EPS)
            unit = unit * scale
            normed = (unit * gain).astype(BF16)
            for kb in range(K // KB):
                block = slice(kb * KB, kb * KB + KB)
                value, slope = gelu_both(mm(cit[block, :], normed))
                inner_s[block, :] = value.astype(BF16)
                slope_s[block, :] = slope
            second = (first + mm(cot[...], inner_s[...])).astype(BF16)
            logits = mm(head16[...], second)[:8]
            target = lanes([tgt[b] for b in at])
            phases = lax.broadcasted_iota(jnp.int32, (8, G * L), 0).astype(F32)
            exps = jnp.exp(logits - jnp.max(logits, axis=0, keepdims=True))
            probs = exps / jnp.sum(exps, axis=0, keepdims=True)
            diff = probs - jnp.where(phases == target, 1.0, 0.0)
            slope16 = jnp.concatenate([diff, jnp.zeros((8, G * L), F32)], axis=0).astype(BF16)
            hp[...] += mm_nt(slope16, second)
            back_second = mm(headc[...], slope16)
            back_low = back_second.astype(BF16)
            for kb in range(K // KB):
                block = slice(kb * KB, kb * KB + KB)
                bip_s[block, :] = (mm(co[block, :], back_low) * slope_s[block, :]).astype(BF16)
            w = mm(ci[...], bip_s[...]) * gain
            back = back_second + scale * (w - mean0(w) - unit * mean0(w * unit))
            low = back.astype(BF16)
            for g in range(G):
                bf[at[g]] = back[:, g * L : (g + 1) * L]
                send3[:, at[g]] = low[:, g * L : (g + 1) * L].reshape(NP, CL, L)

            send_step(2, h, i, send3, recv3)
            return carry

        lax.fori_loop(0, NB // G, body, 0)

    def norm_back(h):
        def body(i, carry):
            b = h * NB + i
            scale = rstd[b]
            unit = (x_s[b].astype(F32) - mu[b]) * scale
            w = recv4[h, :, i].reshape(C, L).astype(F32) * gin[...]
            bf[b] = bf[b] + scale * (w - mean0(w) - unit * mean0(w * unit))
            out_copy(b).start()
            return carry

        lax.fori_loop(0, NB, body, 0)

    def out_copy(b):
        return pltpu.make_async_copy(bf.at[b], out_hbm.at[:, b], out_sem.at[b])

    def line_drain(s, h, part, sibr, zs, zr, hact):
        for i in range(2):
            sib_copy(s, h, part, sibr, i).wait_send()
        for i in range(3):
            z_copy(s, h, zs, zr, i, xor(z, 1), 0).wait_send()
        for d in range(1, 4):
            ag_copy(s, h, hact, d, mine).wait_send()
        for zz in range(4):
            fw_copy(s, h, hact, zz, core).wait_send()

    def ha_copy(i):
        return pltpu.make_async_remote_copy(
            src_ref=hsend.at[0], dst_ref=hbuf_a.at[ag], send_sem=ha_s.at[i], recv_sem=ha_r.at[i],
            device_id={"agent": lax.rem(ag + i, 8), "chan": chan, "batch": batch}, device_id_type=MESH,
        )

    def hy_copy(i):
        return pltpu.make_async_remote_copy(
            src_ref=hsend.at[1], dst_ref=hbuf_y.at[y], send_sem=hy_s.at[i], recv_sem=hy_r.at[i],
            device_id=plane(lax.rem(y + i, 4) * 4 + xx), device_id_type=MESH,
        )

    def hx_copy(i):
        return pltpu.make_async_remote_copy(
            src_ref=hsend.at[2], dst_ref=hbuf_x.at[xx], send_sem=hx_s.at[i], recv_sem=hx_r.at[i],
            device_id=plane(y * 4 + lax.rem(xx + i, 4)), device_id_type=MESH,
        )

    def total(buf, n):
        out = buf[0]
        for i in range(1, n):
            out = out + buf[i]
        return out

    loads[0].wait()
    loads[1].start()

    def samples_first(first, count):
        def body(i, carry):
            piece = pl.ds(pl.multiple_of(i * CL, CL), CL)
            field = x_raw[piece].astype(F32)[:, first : first + count]
            x_s[first : first + count, piece] = jnp.transpose(field, (1, 0, 2)).astype(BF16)
            return carry

        lax.fori_loop(0, NP, body, 0)

    samples_first(0, G)
    norm_in(0, G)
    pl.semaphore_wait(barrier, NP - 1 + 7)
    send_step(0, 0, 0, send1, recv1)
    for i in range(1, NB // G):
        samples_first(i * G, G)
        norm_in(i * G, G)
        send_step(0, 0, i, send1, recv1)
    loads[2].start()
    loads[3].start()
    for h in range(1, NC):
        samples_first(h * NB, NB)
        norm_in(h * NB, NB)
        a2a_drain(0, h - 1, send1, recv1)
        a2a_send(0, h, send1, recv1)
    gmid[...] = jnp.transpose(jnp.broadcast_to(gmid_ref[...], (L, C)))
    head_rows = jnp.concatenate([head_ref[...].astype(F32), jnp.zeros((8, C), F32)], axis=0)
    head16[...] = head_rows.astype(BF16)
    wide_head = jnp.concatenate([head_rows, jnp.zeros((L - 16, C), F32)], axis=0)
    headc[...] = jnp.transpose(wide_head)[:, :16].astype(BF16)
    spot = lax.broadcasted_iota(jnp.int32, (L, L), 0) == lax.rem(ord_ref[...], L)
    targets = mm(act_ref[...].astype(F32).astype(BF16), spot.astype(F32).astype(BF16))
    for b in range(B):
        tgt[b] = targets[b : b + 1, :]
    hp[...] = jnp.zeros((16, C), F32)

    loads[2].wait()
    loads[3].wait()
    for kb in range(4):
        block = slice(kb * 256, kb * 256 + 256)
        cit[block, :] = jnp.transpose(ci[:, block])
        cot[:, block] = jnp.transpose(co[block, :])
    loads[1].wait()
    loads[4].start()
    for h in range(NC):
        a2a_wait(0, h, send1, recv1)
        contract(0, h, recv1, lambda a, block: mm(a, cols(win, block)), part1, sibr1, zs1, zr1)
    for h in range(NC):
        value, slope = gelu_both(summed(0, h, zs1, zr1))
        hact1[h, mine] = value.astype(BF16)
        hslope[h] = slope
        spread(0, h, hact1)
    loads[4].wait()
    for h in range(NC):
        forward(0, h, hact1)
        gather_wait(0, h, hact1)
        expand(1, h, hact1, lambda a, group: mm(a, cols(wout, group * 2)), send2, recv2)
    for h in range(NC):
        a2a_wait(1, h, send2, recv2)
        channel_part(h)
    a2a_drain(0, NC - 1, send1, recv1)
    for h in range(NC):
        line_drain(0, h, part1, sibr1, zs1, zr1, hact1)
        a2a_drain(1, h, send2, recv2)
    hsend[0] = hp[:8]
    hbuf_a[ag] = hp[:8]
    for i in range(1, 8):
        ha_copy(i).start()
    for h in range(NC):
        a2a_wait(2, h, send3, recv3)
        contract(1, h, recv3, lambda a, block: mm_nt(a, rows(wout, block)), part2, sibr2, zs2, zr2)
    for i in range(1, 8):
        ha_copy(i).wait()
    sums = total(hbuf_a, 8)
    hsend[1] = sums
    hbuf_y[y] = sums
    for i in range(1, 4):
        hy_copy(i).start()
    for h in range(NC):
        hact2[h, mine] = (summed(1, h, zs2, zr2) * hslope[h]).astype(BF16)
        spread(1, h, hact2)
    for i in range(1, 4):
        hy_copy(i).wait()
    sums = total(hbuf_y, 4)
    hsend[2] = sums
    hbuf_x[xx] = sums
    for i in range(1, 4):
        hx_copy(i).start()
    for h in range(NC):
        forward(1, h, hact2)
        gather_wait(1, h, hact2)
        expand(3, h, hact2, lambda a, group: mm_nt(a, rows(win, group * 2)), send4, recv4)
    for i in range(1, 4):
        hx_copy(i).wait()
    hg_ref[...] = total(hbuf_x, 4)
    for h in range(NC):
        a2a_drain(2, h, send3, recv3)
        line_drain(1, h, part2, sibr2, zs2, zr2, hact2)
        if h < NC - 1:
            a2a_drain(3, h, send4, recv4)
    for h in range(NC):
        a2a_wait(3, h, send4, recv4)
        norm_back(h)

    a2a_drain(3, NC - 1, send4, recv4)
    for b in range(B):
        out_copy(b).wait()


def fused(x, gin, win, wout, gmid, ci, co, head, actions, order):
    hbm = pl.BlockSpec(memory_space=pl.ANY)
    vmem = pl.BlockSpec(memory_space=pltpu.VMEM)
    dma = pltpu.SemaphoreType.DMA
    V = pltpu.VMEM
    exchange = V((NP, B, CL, L), BF16)
    arrive = V((NC, NP, NB, CL, L), BF16)
    scratch = [
        V((C, B, L), BF16), V((B, C, L), BF16), V((T, J), BF16), V((J, T), BF16),
        V((C, K), BF16), V((K, C), BF16), V((K, C), BF16), V((C, K), BF16),
        V((C, L), F32), V((C, L), F32), V((16, C), BF16), V((C, 16), BF16),
        V((B, 1, L), F32), V((B, 1, L), F32), V((B, 1, L), F32), V((B, C, L), F32),
        exchange, exchange, exchange, exchange, arrive, arrive, arrive, arrive,
        V((NC, 2, R, 2 * Q), BF16), V((NC, 2, R, 2 * Q), BF16),
        V((NC, 2, R, 2 * Q), BF16), V((NC, 2, R, 2 * Q), BF16),
        V((NC, 3, R, Q), BF16), V((NC, 3, R, Q), BF16),
        V((NC, 3, R, Q), BF16), V((NC, 3, R, Q), BF16),
        V((NC, 8, R, Q), BF16), V((NC, 8, R, Q), BF16),
        V((2, NC, 2, R, Q), F32), V((NC, R, Q), F32),
        V((K, G * L), BF16), V((K, G * L), F32), V((K, G * L), BF16), V((16, C), F32),
        V((8, 8, C), F32), V((4, 8, C), F32), V((4, 8, C), F32), V((3, 8, C), F32),
        dma((5,)), dma((B,)), dma((4, NC)), dma((4, NC)),
        dma((2, NC, 2)), dma((2, NC, 2)), dma((2, NC, 3)), dma((2, NC, 3)),
        dma((2, NC, 3)), dma((2, NC, 3)), dma((2, NC, 4)), dma((2, NC, 4)),
        dma((8,)), dma((8,)), dma((4,)), dma((4,)), dma((4,)), dma((4,)),
    ]
    return pl.pallas_call(
        kernel,
        out_shape=(jax.ShapeDtypeStruct((C, B, L), F32), jax.ShapeDtypeStruct((8, C), F32)),
        in_specs=[hbm, vmem, hbm, hbm, vmem, hbm, hbm, vmem, vmem, vmem],
        out_specs=(hbm, vmem),
        scratch_shapes=scratch,
        compiler_params=pltpu.CompilerParams(
            collective_id=0, has_side_effects=True, vmem_limit_bytes=58 << 20
        ),
    )(x, gin, win, wout, gmid, ci, co, head, actions, order)


def hand_over(grad_in, head_in, grad_out, head_out, held, in_sem, out_sem):
    def piece(i):
        return pl.ds(i * (C // PIECES), C // PIECES)

    arrive = [
        pltpu.make_async_copy(grad_in.at[piece(i)], held.at[piece(i)], in_sem.at[i]) for i in range(PIECES)
    ]
    leave = [
        pltpu.make_async_copy(held.at[piece(i)], grad_out.at[piece(i)], out_sem.at[i]) for i in range(PIECES)
    ]
    for copy in arrive:
        copy.start()
    head_out[...] = head_in[...] * (1.0 / (B * A))
    for i in range(PIECES):
        arrive[i].wait()
        leave[i].start()
    for copy in leave:
        copy.wait()


def deliver(grad, head):
    hbm = pl.BlockSpec(memory_space=pl.ANY)
    vmem = pl.BlockSpec(memory_space=pltpu.VMEM)
    return pl.pallas_call(
        hand_over,
        out_shape=(jax.ShapeDtypeStruct((C, B, L), F32), jax.ShapeDtypeStruct((8, C), F32)),
        in_specs=[hbm, vmem],
        out_specs=(hbm, vmem),
        scratch_shapes=[
            pltpu.VMEM((C, B, L), F32),
            pltpu.SemaphoreType.DMA((PIECES,)),
            pltpu.SemaphoreType.DMA((PIECES,)),
        ],
        compiler_params=pltpu.CompilerParams(vmem_limit_bytes=60 << 20),
    )(grad, head)


def shards(features, norm_gain, tok_in, tok_out, mix_gain, chan_in, chan_out, head, actions, order):
    grad, head_grad = fused(
        features,
        norm_gain.reshape(1, C),
        tok_in,
        tok_out,
        mix_gain.reshape(1, C),
        chan_in,
        chan_out,
        head.T,
        actions,
        order.reshape(1, L),
    )
    grad, head_grad = deliver(grad, head_grad)
    return grad, head_grad.T


def solution(mesh):
    in_specs = (
        P(None, None, ("agent", "chan", "batch")),
        P(),
        P("agent", None),
        P(None, "agent"),
        P(),
        P(),
        P(),
        P(),
        P(None, ("agent", "chan", "batch")),
        P(("agent", "chan", "batch")),
    )
    out_specs = (P(None, None, ("agent", "chan", "batch")), P())
    return jax.shard_map(shards, mesh=mesh, in_specs=in_specs, out_specs=out_specs, check_vma=False)
```

```python
import jax
import jax.numpy as jnp
from jax import lax
from jax.experimental import pallas as pl
from jax.experimental.pallas import tpu as pltpu
from jax.sharding import PartitionSpec as P

MESH = pl.DeviceIdType.MESH
F32 = jnp.float32
BF16 = jnp.bfloat16

A = 16384
B = 16
C = 256
L = 128
NP = 16
CL = C // NP
T = NP * L
J = 2048
K = 1024
NC = 2
NB = B // NC
R = NB * CL
G = 4
KB = 256
PIECES = 8
Q = J // 8

GELU_K = 0.7978845608028654
GELU_C = 0.044715
EPS = 1e-05


def mm(a, b):
    return lax.dot_general(a, b, (((1,), (0,)), ((), ())), preferred_element_type=F32)


def mm_nt(a, b):
    return lax.dot_general(a, b, (((1,), (1,)), ((), ())), preferred_element_type=F32)


def gelu_both(v):
    square = v * v
    half = 0.5 + 0.5 * jnp.tanh(v * (GELU_K + (GELU_K * GELU_C) * square))
    value = v * half
    slope = half + value * (1.0 - half) * (2.0 * GELU_K + (6.0 * GELU_K * GELU_C) * square)
    return value, slope


def mean0(v):
    return jnp.sum(v, axis=0, keepdims=True) * (1.0 / C)


def kernel(
    x_hbm, gin_hbm, win_hbm, wout_hbm, gmid_hbm, ci_hbm, co_hbm, head_hbm, act_hbm, ord_hbm,
    out_hbm, hg_ref,
    gin_ref, gmid_ref, head_ref, act_ref, ord_ref, x_raw, x_s, win, wout, ci, co, cit, cot, gin, gmid, head16, headc, tgt, mu, rstd, bf,
    send1, send2, send3, send4, recv1, recv2, recv3, recv4,
    part1, part2, sibr1, sibr2, zs1, zs2, zr1, zr2, hact1, hact2, ownp, hslope,
    inner_s, slope_s, bip_s, hp, hbuf_a, hbuf_y, hbuf_x, hsend,
    ld_sem, out_sem, a2a_s, a2a_r, sib_s, sib_r, z_s, z_r, ag_s, ag_r, fw_s, fw_r,
    ha_s, ha_r, hy_s, hy_r, hx_s, hx_r,
):
    ag = lax.axis_index("agent")
    chan = lax.axis_index("chan")
    batch = lax.axis_index("batch")
    me = chan * 2 + batch
    z = ag // 2
    core = lax.rem(ag, 2)
    y = me // 4
    xx = lax.rem(me, 4)
    mine = core * 4 + z

    def plane(p):
        return {"agent": ag, "chan": p // 2, "batch": lax.rem(p, 2)}

    def line(zz, cc):
        return {"agent": zz * 2 + cc, "chan": chan, "batch": batch}

    def xor(a, d):
        out = a
        if d & 1:
            out = out + 1 - 2 * lax.rem(out, 2)
        if d & 2:
            out = lax.rem(out + 2, 4)
        return out

    loads = [
        pltpu.make_async_copy(x_hbm, x_raw, ld_sem.at[0]),
        pltpu.make_async_copy(win_hbm, win, ld_sem.at[1]),
        pltpu.make_async_copy(ci_hbm, ci, ld_sem.at[2]),
        pltpu.make_async_copy(co_hbm, co, ld_sem.at[3]),
        pltpu.make_async_copy(wout_hbm, wout, ld_sem.at[4]),
        pltpu.make_async_copy(gin_hbm, gin_ref, ld_sem.at[5]),
        pltpu.make_async_copy(gmid_hbm, gmid_ref, ld_sem.at[6]),
        pltpu.make_async_copy(head_hbm, head_ref, ld_sem.at[7]),
        pltpu.make_async_copy(act_hbm, act_ref, ld_sem.at[8]),
        pltpu.make_async_copy(ord_hbm, ord_ref, ld_sem.at[9]),
    ]
    loads[5].start()
    loads[0].start()
    for load in loads[6:]:
        load.start()

    barrier = pltpu.get_barrier_semaphore()
    for i in range(1, NP):
        pl.semaphore_signal(barrier, inc=1, device_id=plane(lax.rem(me + i, NP)), device_id_type=MESH)
    for i in range(1, 8):
        pl.semaphore_signal(
            barrier, inc=1,
            device_id={"agent": lax.rem(ag + i, 8), "chan": chan, "batch": batch},
            device_id_type=MESH,
        )

    loads[5].wait()
    gin[...] = jnp.transpose(jnp.broadcast_to(gin_ref[...], (L, C)))

    def a2a_copy(k, h, send, recv, p, slot):
        return pltpu.make_async_remote_copy(
            src_ref=send.at[p, pl.ds(h * NB, NB)],
            dst_ref=recv.at[h, slot],
            send_sem=a2a_s.at[k, h],
            recv_sem=a2a_r.at[k, h],
            device_id=plane(p),
            device_id_type=MESH,
        )

    def a2a_send(k, h, send, recv):
        def body(i, carry):
            a2a_copy(k, h, send, recv, lax.rem(me + i, NP), me).start()
            return carry

        lax.fori_loop(1, NP, body, 0)

    def send_step(k, h, i, send, recv):
        def body(d, carry):
            p = lax.rem(me + d, NP)
            pltpu.make_async_remote_copy(
                src_ref=send.at[p, pl.ds(h * NB + i * G, G)],
                dst_ref=recv.at[h, me, pl.ds(i * G, G)],
                send_sem=a2a_s.at[k, h],
                recv_sem=a2a_r.at[k, h],
                device_id=plane(p),
                device_id_type=MESH,
            ).start()
            return carry

        lax.fori_loop(1, NP, body, 0)

    def a2a_wait(k, h, send, recv):
        recv[h, me] = send[me, pl.ds(h * NB, NB)]
        others = recv.at[h, pl.ds(0, NP - 1)]
        pltpu.make_async_copy(others, others, a2a_r.at[k, h]).wait()

    def a2a_drain(k, h, send, recv):
        others = recv.at[h, pl.ds(0, NP - 1)]
        pltpu.make_async_copy(others, others, a2a_s.at[k, h]).wait()

    def sib_copy(s, h, part, sibr, i):
        return pltpu.make_async_remote_copy(
            src_ref=part.at[h, i], dst_ref=sibr.at[h, i],
            send_sem=sib_s.at[s, h, i], recv_sem=sib_r.at[s, h, i],
            device_id=line(z, 1 - core), device_id_type=MESH,
        )

    def z_copy(s, h, zs, zr, src, zz, slot):
        return pltpu.make_async_remote_copy(
            src_ref=zs.at[h, src], dst_ref=zr.at[h, slot],
            send_sem=z_s.at[s, h, src], recv_sem=z_r.at[s, h, slot],
            device_id=line(zz, core), device_id_type=MESH,
        )

    def ag_copy(s, h, hact, d, block):
        return pltpu.make_async_remote_copy(
            src_ref=hact.at[h, block], dst_ref=hact.at[h, block],
            send_sem=ag_s.at[s, h, d - 1], recv_sem=ag_r.at[s, h, d - 1],
            device_id=line(xor(z, d), core), device_id_type=MESH,
        )

    def fw_copy(s, h, hact, zz, cc):
        return pltpu.make_async_remote_copy(
            src_ref=hact.at[h, cc * 4 + zz], dst_ref=hact.at[h, cc * 4 + zz],
            send_sem=fw_s.at[s, h, zz], recv_sem=fw_r.at[s, h, zz],
            device_id=line(z, 1 - core), device_id_type=MESH,
        )

    def rows_of(recv, h):
        return jnp.concatenate([recv[h, p].reshape(R, L) for p in range(NP)], axis=1)

    def contract(s, h, recv, product, part, sibr, zs, zr):
        def for_sibling(i, carry):
            part[h, i] = product(rows_of(recv, h), (1 - core) * 4 + 2 * i).astype(BF16)
            sib_copy(s, h, part, sibr, i).start()
            return carry

        lax.fori_loop(0, 2, for_sibling, 0)
        half = z // 2
        other = 1 - half
        far = product(rows_of(recv, h), core * 4 + 2 * other)
        sib_copy(s, h, part, sibr, other).wait_recv()
        far = far + sibr[h, other].astype(F32)
        zs[h, 0] = far[:, :Q].astype(BF16)
        zs[h, 1] = far[:, Q:].astype(BF16)
        low = lax.rem(z, 2)
        z_copy(s, h, zs, zr, low, xor(z, 2), 1).start()
        z_copy(s, h, zs, zr, 1 - low, xor(z, 3), 2).start()
        near = product(rows_of(recv, h), core * 4 + 2 * half)
        sib_copy(s, h, part, sibr, half).wait_recv()
        near = near + sibr[h, half].astype(F32)
        ownp[s, h, 0] = near[:, :Q]
        ownp[s, h, 1] = near[:, Q:]
        zs[h, 2] = ownp[s, h, 1 - low].astype(BF16)
        z_copy(s, h, zs, zr, 2, xor(z, 1), 0).start()

    def summed(s, h, zs, zr):
        low = lax.rem(z, 2)
        total = ownp[s, h, low]
        for d in range(1, 4):
            z_copy(s, h, zs, zr, 0, xor(z, d), d - 1).wait_recv()
            total = total + zr[h, d - 1].astype(F32)
        return total

    def spread(s, h, hact):
        for d in range(1, 4):
            ag_copy(s, h, hact, d, mine).start()
        fw_copy(s, h, hact, z, core).start()

    def forward(s, h, hact):
        for d in (1, 3, 2):
            zz = xor(z, d)
            ag_copy(s, h, hact, d, core * 4 + zz).wait_recv()
            fw_copy(s, h, hact, zz, core).start()

    def gather_wait(s, h, hact):
        for zz in range(4):
            fw_copy(s, h, hact, zz, 1 - core).wait_recv()

    def expand(k, h, hact, product, send, recv):
        def store(tile, group):
            for i in range(4):
                send[group * 4 + i, pl.ds(h * NB, NB)] = tile[:, i * L : (i + 1) * L].reshape(NB, CL, L)

        def row_of(group):
            rows = jnp.concatenate([hact[h, q] for q in range(8)], axis=1)
            store(product(rows, group).astype(BF16), group)

        def body(t, carry):
            group = lax.rem(y + 1 + t, 4)
            row_of(group)
            for i in range(4):
                p = group * 4 + lax.rem(xx + i, 4)
                a2a_copy(k, h, send, recv, p, me).start()
            return carry

        lax.fori_loop(0, 3, body, 0)
        row_of(y)
        for i in range(1, 4):
            a2a_copy(k, h, send, recv, y * 4 + lax.rem(xx + i, 4), me).start()

    def cols(w, block):
        return w[:, pl.ds(pl.multiple_of(block * Q, Q), 2 * Q)]

    def rows(w, block):
        return w[pl.ds(pl.multiple_of(block * Q, Q), 2 * Q), :]

    def norm_in(first, count):
        def body(i, carry):
            b = first + i
            field = x_s[b].astype(F32)
            center = mean0(field)
            field = field - center
            scale = lax.rsqrt(mean0(field * field) + EPS)
            mu[b] = center
            rstd[b] = scale
            send1[:, b] = (field * scale * gin[...]).astype(BF16).reshape(NP, CL, L)
            return carry

        lax.fori_loop(0, count, body, 0)

    def channel_part(h):
        def body(i, carry):
            local = [G * i + g for g in range(G)]
            at = [h * NB + b for b in local]

            def lanes(pieces):
                return jnp.concatenate(pieces, axis=1)

            wide = lanes([x_s[b] for b in at]).astype(F32)
            mixed = lanes([recv2[h, :, b].reshape(C, L) for b in local])
            first = wide + mixed.astype(F32)
            gain = lanes([gmid[...]] * G)
            center = mean0(first)
            unit = first - center
            scale = lax.rsqrt(mean0(unit * unit) + EPS)
            unit = unit * scale
            normed = (unit * gain).astype(BF16)
            for kb in range(K // KB):
                block = slice(kb * KB, kb * KB + KB)
                value, slope = gelu_both(mm(cit[block, :], normed))
                inner_s[block, :] = value.astype(BF16)
                slope_s[block, :] = slope
            second = (first + mm(cot[...], inner_s[...])).astype(BF16)
            logits = mm(head16[...], second)[:8]
            target = lanes([tgt[b] for b in at])
            phases = lax.broadcasted_iota(jnp.int32, (8, G * L), 0).astype(F32)
            exps = jnp.exp(logits - jnp.max(logits, axis=0, keepdims=True))
            probs = exps / jnp.sum(exps, axis=0, keepdims=True)
            diff = probs - jnp.where(phases == target, 1.0, 0.0)
            slope16 = jnp.concatenate([diff, jnp.zeros((8, G * L), F32)], axis=0).astype(BF16)
            hp[...] += mm_nt(slope16, second)
            back_second = mm(headc[...], slope16)
            back_low = back_second.astype(BF16)
            for kb in range(K // KB):
                block = slice(kb * KB, kb * KB + KB)
                bip_s[block, :] = (mm(co[block, :], back_low) * slope_s[block, :]).astype(BF16)
            w = mm(ci[...], bip_s[...]) * gain
            back = back_second + scale * (w - mean0(w) - unit * mean0(w * unit))
            low = back.astype(BF16)
            for g in range(G):
                bf[at[g]] = back[:, g * L : (g + 1) * L]
                send3[:, at[g]] = low[:, g * L : (g + 1) * L].reshape(NP, CL, L)

            send_step(2, h, i, send3, recv3)
            return carry

        lax.fori_loop(0, NB // G, body, 0)

    def norm_back(h):
        def body(i, carry):
            b = h * NB + i
            scale = rstd[b]
            unit = (x_s[b].astype(F32) - mu[b]) * scale
            w = recv4[h, :, i].reshape(C, L).astype(F32) * gin[...]
            bf[b] = bf[b] + scale * (w - mean0(w) - unit * mean0(w * unit))
            out_copy(b).start()
            return carry

        lax.fori_loop(0, NB, body, 0)

    def out_copy(b):
        return pltpu.make_async_copy(bf.at[b], out_hbm.at[:, b], out_sem.at[b])

    def line_drain(s, h, part, sibr, zs, zr, hact):
        for i in range(2):
            sib_copy(s, h, part, sibr, i).wait_send()
        for i in range(3):
            z_copy(s, h, zs, zr, i, xor(z, 1), 0).wait_send()
        for d in range(1, 4):
            ag_copy(s, h, hact, d, mine).wait_send()
        for zz in range(4):
            fw_copy(s, h, hact, zz, core).wait_send()

    def ha_copy(i):
        return pltpu.make_async_remote_copy(
            src_ref=hsend.at[0], dst_ref=hbuf_a.at[ag], send_sem=ha_s.at[i], recv_sem=ha_r.at[i],
            device_id={"agent": lax.rem(ag + i, 8), "chan": chan, "batch": batch}, device_id_type=MESH,
        )

    def hy_copy(i):
        return pltpu.make_async_remote_copy(
            src_ref=hsend.at[1], dst_ref=hbuf_y.at[y], send_sem=hy_s.at[i], recv_sem=hy_r.at[i],
            device_id=plane(lax.rem(y + i, 4) * 4 + xx), device_id_type=MESH,
        )

    def hx_copy(i):
        return pltpu.make_async_remote_copy(
            src_ref=hsend.at[2], dst_ref=hbuf_x.at[xx], send_sem=hx_s.at[i], recv_sem=hx_r.at[i],
            device_id=plane(y * 4 + lax.rem(xx + i, 4)), device_id_type=MESH,
        )

    def total(buf, n):
        out = buf[0]
        for i in range(1, n):
            out = out + buf[i]
        return out

    loads[0].wait()
    loads[1].start()

    def samples_first(first, count):
        def body(i, carry):
            piece = pl.ds(pl.multiple_of(i * CL, CL), CL)
            field = x_raw[piece].astype(F32)[:, first : first + count]
            x_s[first : first + count, piece] = jnp.transpose(field, (1, 0, 2)).astype(BF16)
            return carry

        lax.fori_loop(0, NP, body, 0)

    samples_first(0, G)
    norm_in(0, G)
    pl.semaphore_wait(barrier, NP - 1 + 7)
    send_step(0, 0, 0, send1, recv1)
    for i in range(1, NB // G):
        samples_first(i * G, G)
        norm_in(i * G, G)
        send_step(0, 0, i, send1, recv1)
    loads[2].start()
    loads[3].start()
    for h in range(1, NC):
        samples_first(h * NB, NB)
        norm_in(h * NB, NB)
        a2a_drain(0, h - 1, send1, recv1)
        a2a_send(0, h, send1, recv1)
    for load in loads[6:]:
        load.wait()
    gmid[...] = jnp.transpose(jnp.broadcast_to(gmid_ref[...], (L, C)))
    head_rows = jnp.concatenate([head_ref[...].astype(F32), jnp.zeros((8, C), F32)], axis=0)
    head16[...] = head_rows.astype(BF16)
    wide_head = jnp.concatenate([head_rows, jnp.zeros((L - 16, C), F32)], axis=0)
    headc[...] = jnp.transpose(wide_head)[:, :16].astype(BF16)
    spot = lax.broadcasted_iota(jnp.int32, (L, L), 0) == lax.rem(ord_ref[...], L)
    targets = mm(act_ref[...].astype(F32).astype(BF16), spot.astype(F32).astype(BF16))
    for b in range(B):
        tgt[b] = targets[b : b + 1, :]
    hp[...] = jnp.zeros((16, C), F32)

    loads[2].wait()
    loads[3].wait()
    for kb in range(4):
        block = slice(kb * 256, kb * 256 + 256)
        cit[block, :] = jnp.transpose(ci[:, block])
        cot[:, block] = jnp.transpose(co[block, :])
    loads[1].wait()
    loads[4].start()
    for h in range(NC):
        a2a_wait(0, h, send1, recv1)
        contract(0, h, recv1, lambda a, block: mm(a, cols(win, block)), part1, sibr1, zs1, zr1)
    for h in range(NC):
        value, slope = gelu_both(summed(0, h, zs1, zr1))
        hact1[h, mine] = value.astype(BF16)
        hslope[h] = slope
        spread(0, h, hact1)
    loads[4].wait()
    for h in range(NC):
        forward(0, h, hact1)
        gather_wait(0, h, hact1)
        expand(1, h, hact1, lambda a, group: mm(a, cols(wout, group * 2)), send2, recv2)
    for h in range(NC):
        a2a_wait(1, h, send2, recv2)
        channel_part(h)
    a2a_drain(0, NC - 1, send1, recv1)
    for h in range(NC):
        line_drain(0, h, part1, sibr1, zs1, zr1, hact1)
        a2a_drain(1, h, send2, recv2)
    hsend[0] = hp[:8]
    hbuf_a[ag] = hp[:8]
    for i in range(1, 8):
        ha_copy(i).start()
    for h in range(NC):
        a2a_wait(2, h, send3, recv3)
        contract(1, h, recv3, lambda a, block: mm_nt(a, rows(wout, block)), part2, sibr2, zs2, zr2)
    for i in range(1, 8):
        ha_copy(i).wait()
    sums = total(hbuf_a, 8)
    hsend[1] = sums
    hbuf_y[y] = sums
    for i in range(1, 4):
        hy_copy(i).start()
    for h in range(NC):
        hact2[h, mine] = (summed(1, h, zs2, zr2) * hslope[h]).astype(BF16)
        spread(1, h, hact2)
    for i in range(1, 4):
        hy_copy(i).wait()
    sums = total(hbuf_y, 4)
    hsend[2] = sums
    hbuf_x[xx] = sums
    for i in range(1, 4):
        hx_copy(i).start()
    for h in range(NC):
        forward(1, h, hact2)
        gather_wait(1, h, hact2)
        expand(3, h, hact2, lambda a, group: mm_nt(a, rows(win, group * 2)), send4, recv4)
    for i in range(1, 4):
        hx_copy(i).wait()
    hg_ref[...] = total(hbuf_x, 4)
    for h in range(NC):
        a2a_drain(2, h, send3, recv3)
        line_drain(1, h, part2, sibr2, zs2, zr2, hact2)
        if h < NC - 1:
            a2a_drain(3, h, send4, recv4)
    for h in range(NC):
        a2a_wait(3, h, send4, recv4)
        norm_back(h)

    a2a_drain(3, NC - 1, send4, recv4)
    for b in range(B):
        out_copy(b).wait()


def fused(x, gin, win, wout, gmid, ci, co, head, actions, order):
    hbm = pl.BlockSpec(memory_space=pl.ANY)
    vmem = pl.BlockSpec(memory_space=pltpu.VMEM)
    dma = pltpu.SemaphoreType.DMA
    V = pltpu.VMEM
    exchange = V((NP, B, CL, L), BF16)
    arrive = V((NC, NP, NB, CL, L), BF16)
    scratch = [
        V((1, C), F32), V((1, C), F32), V((8, C), BF16), V((B, L), jnp.int32), V((1, L), jnp.int32),
        V((C, B, L), BF16), V((B, C, L), BF16), V((T, J), BF16), V((J, T), BF16),
        V((C, K), BF16), V((K, C), BF16), V((K, C), BF16), V((C, K), BF16),
        V((C, L), F32), V((C, L), F32), V((16, C), BF16), V((C, 16), BF16),
        V((B, 1, L), F32), V((B, 1, L), F32), V((B, 1, L), F32), V((B, C, L), F32),
        exchange, exchange, exchange, exchange, arrive, arrive, arrive, arrive,
        V((NC, 2, R, 2 * Q), BF16), V((NC, 2, R, 2 * Q), BF16),
        V((NC, 2, R, 2 * Q), BF16), V((NC, 2, R, 2 * Q), BF16),
        V((NC, 3, R, Q), BF16), V((NC, 3, R, Q), BF16),
        V((NC, 3, R, Q), BF16), V((NC, 3, R, Q), BF16),
        V((NC, 8, R, Q), BF16), V((NC, 8, R, Q), BF16),
        V((2, NC, 2, R, Q), F32), V((NC, R, Q), F32),
        V((K, G * L), BF16), V((K, G * L), F32), V((K, G * L), BF16), V((16, C), F32),
        V((8, 8, C), F32), V((4, 8, C), F32), V((4, 8, C), F32), V((3, 8, C), F32),
        dma((10,)), dma((B,)), dma((4, NC)), dma((4, NC)),
        dma((2, NC, 2)), dma((2, NC, 2)), dma((2, NC, 3)), dma((2, NC, 3)),
        dma((2, NC, 3)), dma((2, NC, 3)), dma((2, NC, 4)), dma((2, NC, 4)),
        dma((8,)), dma((8,)), dma((4,)), dma((4,)), dma((4,)), dma((4,)),
    ]
    return pl.pallas_call(
        kernel,
        out_shape=(jax.ShapeDtypeStruct((C, B, L), F32), jax.ShapeDtypeStruct((8, C), F32)),
        in_specs=[pl.BlockSpec(memory_space=pltpu.HBM)] * 10,
        out_specs=(hbm, vmem),
        scratch_shapes=scratch,
        compiler_params=pltpu.CompilerParams(
            collective_id=0, has_side_effects=True, vmem_limit_bytes=46 << 20
        ),
    )(*[pltpu.with_memory_space_constraint(v, pltpu.HBM) for v in (x, gin, win, wout, gmid, ci, co, head, actions, order)])


def hand_over(grad_in, head_in, grad_out, head_out, sem):
    copies = []
    for i in range(PIECES):
        piece = pl.ds(i * (C // PIECES), C // PIECES)
        copies.append(pltpu.make_async_copy(grad_in.at[piece], grad_out.at[piece], sem.at[i]))
        copies[-1].start()
    head_out[...] = head_in[...] * (1.0 / (B * A))
    for copy in copies:
        copy.wait()


def deliver(grad, head):
    hbm = pl.BlockSpec(memory_space=pl.ANY)
    vmem = pl.BlockSpec(memory_space=pltpu.VMEM)
    return pl.pallas_call(
        hand_over,
        out_shape=(jax.ShapeDtypeStruct((C, B, L), F32), jax.ShapeDtypeStruct((8, C), F32)),
        in_specs=[hbm, vmem],
        out_specs=(hbm, vmem),
        scratch_shapes=[pltpu.SemaphoreType.DMA((PIECES,))],
        compiler_params=pltpu.CompilerParams(vmem_limit_bytes=8 << 20),
    )(grad, head)


def shards(features, norm_gain, tok_in, tok_out, mix_gain, chan_in, chan_out, head, actions, order):
    grad, head_grad = fused(
        features,
        norm_gain.reshape(1, C),
        tok_in,
        tok_out,
        mix_gain.reshape(1, C),
        chan_in,
        chan_out,
        head.T,
        actions,
        order.reshape(1, L),
    )
    grad, head_grad = deliver(grad, head_grad)
    return grad, head_grad.T


def solution(mesh):
    in_specs = (
        P(None, None, ("agent", "chan", "batch")),
        P(),
        P("agent", None),
        P(None, "agent"),
        P(),
        P(),
        P(),
        P(),
        P(None, ("agent", "chan", "batch")),
        P(("agent", "chan", "batch")),
    )
    out_specs = (P(None, None, ("agent", "chan", "batch")), P())
    return jax.shard_map(shards, mesh=mesh, in_specs=in_specs, out_specs=out_specs, check_vma=False)
```

```python
import jax
import jax.numpy as jnp
from jax import lax
from jax.experimental import pallas as pl
from jax.experimental.pallas import tpu as pltpu
from jax.sharding import PartitionSpec as P

MESH = pl.DeviceIdType.MESH
F32 = jnp.float32
BF16 = jnp.bfloat16

A = 16384
B = 16
C = 256
L = 128
NP = 16
CL = C // NP
T = NP * L
J = 2048
K = 1024
NC = 2
NB = B // NC
R = NB * CL
G = 4
KB = 256
PIECES = 8
Q = J // 8

GELU_K = 0.7978845608028654
GELU_C = 0.044715
EPS = 1e-05


def mm(a, b):
    return lax.dot_general(a, b, (((1,), (0,)), ((), ())), preferred_element_type=F32)


def mm_nt(a, b):
    return lax.dot_general(a, b, (((1,), (1,)), ((), ())), preferred_element_type=F32)


def gelu_both(v):
    square = v * v
    half = 0.5 + 0.5 * jnp.tanh(v * (GELU_K + (GELU_K * GELU_C) * square))
    value = v * half
    slope = half + value * (1.0 - half) * (2.0 * GELU_K + (6.0 * GELU_K * GELU_C) * square)
    return value, slope


def mean0(v):
    return jnp.sum(v, axis=0, keepdims=True) * (1.0 / C)


def kernel(
    x_hbm, gin_hbm, win_hbm, wout_hbm, gmid_hbm, ci_hbm, co_hbm, head_hbm, act_hbm, ord_hbm,
    out_hbm, hg_ref,
    gin_ref, gmid_ref, head_ref, act_ref, ord_ref, x_raw, x_s, win, wout, ci, co, cit, cot, gin, gmid, head16, headc, tgt, mu, rstd, bf,
    send1, send2, send3, send4, recv1, recv2, recv3, recv4,
    part1, part2, sibr1, sibr2, zs1, zs2, zr1, zr2, hact1, hact2, ownp, hslope,
    inner_s, slope_s, bip_s, hp, hbuf_a, hbuf_y, hbuf_x, hsend,
    ld_sem, out_sem, a2a_s, a2a_r, sib_s, sib_r, z_s, z_r, ag_s, ag_r, fw_s, fw_r,
    ha_s, ha_r, hy_s, hy_r, hx_s, hx_r,
):
    ag = lax.axis_index("agent")
    chan = lax.axis_index("chan")
    batch = lax.axis_index("batch")
    me = chan * 2 + batch
    z = ag // 2
    core = lax.rem(ag, 2)
    y = me // 4
    xx = lax.rem(me, 4)
    mine = core * 4 + z

    def plane(p):
        return {"agent": ag, "chan": p // 2, "batch": lax.rem(p, 2)}

    def line(zz, cc):
        return {"agent": zz * 2 + cc, "chan": chan, "batch": batch}

    def xor(a, d):
        out = a
        if d & 1:
            out = out + 1 - 2 * lax.rem(out, 2)
        if d & 2:
            out = lax.rem(out + 2, 4)
        return out

    loads = [
        pltpu.make_async_copy(x_hbm, x_raw, ld_sem.at[0]),
        pltpu.make_async_copy(win_hbm, win, ld_sem.at[1]),
        pltpu.make_async_copy(ci_hbm, ci, ld_sem.at[2]),
        pltpu.make_async_copy(co_hbm, co, ld_sem.at[3]),
        pltpu.make_async_copy(wout_hbm, wout, ld_sem.at[4]),
        pltpu.make_async_copy(gin_hbm, gin_ref, ld_sem.at[5]),
        pltpu.make_async_copy(gmid_hbm, gmid_ref, ld_sem.at[6]),
        pltpu.make_async_copy(head_hbm, head_ref, ld_sem.at[7]),
        pltpu.make_async_copy(act_hbm, act_ref, ld_sem.at[8]),
        pltpu.make_async_copy(ord_hbm, ord_ref, ld_sem.at[9]),
    ]
    loads[5].start()
    loads[0].start()
    for load in loads[6:]:
        load.start()

    barrier = pltpu.get_barrier_semaphore()
    for i in range(1, NP):
        pl.semaphore_signal(barrier, inc=1, device_id=plane(lax.rem(me + i, NP)), device_id_type=MESH)
    for i in range(1, 8):
        pl.semaphore_signal(
            barrier, inc=1,
            device_id={"agent": lax.rem(ag + i, 8), "chan": chan, "batch": batch},
            device_id_type=MESH,
        )

    loads[5].wait()
    gin[...] = jnp.transpose(jnp.broadcast_to(gin_ref[...], (L, C)))

    def a2a_copy(k, h, send, recv, p, slot):
        return pltpu.make_async_remote_copy(
            src_ref=send.at[p, pl.ds(h * NB, NB)],
            dst_ref=recv.at[h, slot],
            send_sem=a2a_s.at[k, h],
            recv_sem=a2a_r.at[k, h],
            device_id=plane(p),
            device_id_type=MESH,
        )

    def a2a_send(k, h, send, recv):
        def body(i, carry):
            a2a_copy(k, h, send, recv, lax.rem(me + i, NP), me).start()
            return carry

        lax.fori_loop(1, NP, body, 0)

    def send_step(k, h, i, send, recv):
        def body(d, carry):
            p = lax.rem(me + d, NP)
            pltpu.make_async_remote_copy(
                src_ref=send.at[p, pl.ds(h * NB + i * G, G)],
                dst_ref=recv.at[h, me, pl.ds(i * G, G)],
                send_sem=a2a_s.at[k, h],
                recv_sem=a2a_r.at[k, h],
                device_id=plane(p),
                device_id_type=MESH,
            ).start()
            return carry

        lax.fori_loop(1, NP, body, 0)

    def a2a_wait(k, h, send, recv):
        recv[h, me] = send[me, pl.ds(h * NB, NB)]
        others = recv.at[h, pl.ds(0, NP - 1)]
        pltpu.make_async_copy(others, others, a2a_r.at[k, h]).wait()

    def a2a_drain(k, h, send, recv):
        others = recv.at[h, pl.ds(0, NP - 1)]
        pltpu.make_async_copy(others, others, a2a_s.at[k, h]).wait()

    def sib_copy(s, h, part, sibr, i):
        return pltpu.make_async_remote_copy(
            src_ref=part.at[h, i], dst_ref=sibr.at[h, i],
            send_sem=sib_s.at[s, h, i], recv_sem=sib_r.at[s, h, i],
            device_id=line(z, 1 - core), device_id_type=MESH,
        )

    def z_copy(s, h, zs, zr, src, zz, slot):
        return pltpu.make_async_remote_copy(
            src_ref=zs.at[h, src], dst_ref=zr.at[h, slot],
            send_sem=z_s.at[s, h, src], recv_sem=z_r.at[s, h, slot],
            device_id=line(zz, core), device_id_type=MESH,
        )

    def ag_copy(s, h, hact, d, block):
        return pltpu.make_async_remote_copy(
            src_ref=hact.at[h, block], dst_ref=hact.at[h, block],
            send_sem=ag_s.at[s, h, d - 1], recv_sem=ag_r.at[s, h, d - 1],
            device_id=line(xor(z, d), core), device_id_type=MESH,
        )

    def fw_copy(s, h, hact, zz, cc):
        return pltpu.make_async_remote_copy(
            src_ref=hact.at[h, cc * 4 + zz], dst_ref=hact.at[h, cc * 4 + zz],
            send_sem=fw_s.at[s, h, zz], recv_sem=fw_r.at[s, h, zz],
            device_id=line(z, 1 - core), device_id_type=MESH,
        )

    def rows_of(recv, h):
        return jnp.concatenate([recv[h, p].reshape(R, L) for p in range(NP)], axis=1)

    def contract(s, h, recv, product, part, sibr, zs, zr):
        half = z // 2
        other = 1 - half
        for i in (other, half):
            part[h, i] = product(rows_of(recv, h), (1 - core) * 4 + 2 * i).astype(BF16)
            sib_copy(s, h, part, sibr, i).start()
        far = product(rows_of(recv, h), core * 4 + 2 * other)
        sib_copy(s, h, part, sibr, other).wait_recv()
        far = far + sibr[h, other].astype(F32)
        zs[h, 0] = far[:, :Q].astype(BF16)
        zs[h, 1] = far[:, Q:].astype(BF16)
        low = lax.rem(z, 2)
        z_copy(s, h, zs, zr, low, xor(z, 2), 1).start()
        z_copy(s, h, zs, zr, 1 - low, xor(z, 3), 2).start()
        near = product(rows_of(recv, h), core * 4 + 2 * half)
        sib_copy(s, h, part, sibr, half).wait_recv()
        near = near + sibr[h, half].astype(F32)
        ownp[s, h, 0] = near[:, :Q]
        ownp[s, h, 1] = near[:, Q:]
        zs[h, 2] = ownp[s, h, 1 - low].astype(BF16)
        z_copy(s, h, zs, zr, 2, xor(z, 1), 0).start()

    def summed(s, h, zs, zr):
        low = lax.rem(z, 2)
        total = ownp[s, h, low]
        for d in range(1, 4):
            z_copy(s, h, zs, zr, 0, xor(z, d), d - 1).wait_recv()
            total = total + zr[h, d - 1].astype(F32)
        return total

    def spread(s, h, hact):
        for d in range(1, 4):
            ag_copy(s, h, hact, d, mine).start()
        fw_copy(s, h, hact, z, core).start()

    def forward(s, h, hact):
        for d in (1, 3, 2):
            zz = xor(z, d)
            ag_copy(s, h, hact, d, core * 4 + zz).wait_recv()
            fw_copy(s, h, hact, zz, core).start()

    def gather_wait(s, h, hact):
        for zz in range(4):
            fw_copy(s, h, hact, zz, 1 - core).wait_recv()

    def expand(k, h, hact, product, send, recv):
        def store(tile, group):
            for i in range(4):
                send[group * 4 + i, pl.ds(h * NB, NB)] = tile[:, i * L : (i + 1) * L].reshape(NB, CL, L)

        def row_of(group):
            rows = jnp.concatenate([hact[h, q] for q in range(8)], axis=1)
            store(product(rows, group).astype(BF16), group)

        def body(t, carry):
            group = lax.rem(y + 1 + t, 4)
            row_of(group)
            for i in range(4):
                p = group * 4 + lax.rem(xx + i, 4)
                a2a_copy(k, h, send, recv, p, me).start()
            return carry

        lax.fori_loop(0, 3, body, 0)
        row_of(y)
        for i in range(1, 4):
            a2a_copy(k, h, send, recv, y * 4 + lax.rem(xx + i, 4), me).start()

    def cols(w, block):
        return w[:, pl.ds(pl.multiple_of(block * Q, Q), 2 * Q)]

    def rows(w, block):
        return w[pl.ds(pl.multiple_of(block * Q, Q), 2 * Q), :]

    def norm_in(first, count):
        def body(i, carry):
            b = first + i
            field = x_s[b].astype(F32)
            center = mean0(field)
            field = field - center
            scale = lax.rsqrt(mean0(field * field) + EPS)
            mu[b] = center
            rstd[b] = scale
            send1[:, b] = (field * scale * gin[...]).astype(BF16).reshape(NP, CL, L)
            return carry

        lax.fori_loop(0, count, body, 0)

    def channel_part(h):
        def body(i, carry):
            local = [G * i + g for g in range(G)]
            at = [h * NB + b for b in local]

            def lanes(pieces):
                return jnp.concatenate(pieces, axis=1)

            wide = lanes([x_s[b] for b in at]).astype(F32)
            mixed = lanes([recv2[h, :, b].reshape(C, L) for b in local])
            first = wide + mixed.astype(F32)
            gain = lanes([gmid[...]] * G)
            center = mean0(first)
            unit = first - center
            scale = lax.rsqrt(mean0(unit * unit) + EPS)
            unit = unit * scale
            normed = (unit * gain).astype(BF16)
            for kb in range(K // KB):
                block = slice(kb * KB, kb * KB + KB)
                value, slope = gelu_both(mm(cit[block, :], normed))
                inner_s[block, :] = value.astype(BF16)
                slope_s[block, :] = slope
            second = (first + mm(cot[...], inner_s[...])).astype(BF16)
            logits = mm(head16[...], second)[:8]
            target = lanes([tgt[b] for b in at])
            phases = lax.broadcasted_iota(jnp.int32, (8, G * L), 0).astype(F32)
            exps = jnp.exp(logits - jnp.max(logits, axis=0, keepdims=True))
            probs = exps / jnp.sum(exps, axis=0, keepdims=True)
            diff = probs - jnp.where(phases == target, 1.0, 0.0)
            slope16 = jnp.concatenate([diff, jnp.zeros((8, G * L), F32)], axis=0).astype(BF16)
            hp[...] += mm_nt(slope16, second)
            back_second = mm(headc[...], slope16)
            back_low = back_second.astype(BF16)
            for kb in range(K // KB):
                block = slice(kb * KB, kb * KB + KB)
                bip_s[block, :] = (mm(co[block, :], back_low) * slope_s[block, :]).astype(BF16)
            w = mm(ci[...], bip_s[...]) * gain
            back = back_second + scale * (w - mean0(w) - unit * mean0(w * unit))
            low = back.astype(BF16)
            for g in range(G):
                bf[at[g]] = back[:, g * L : (g + 1) * L]
                send3[:, at[g]] = low[:, g * L : (g + 1) * L].reshape(NP, CL, L)

            send_step(2, h, i, send3, recv3)
            return carry

        lax.fori_loop(0, NB // G, body, 0)

    def norm_back(h):
        def body(i, carry):
            b = h * NB + i
            scale = rstd[b]
            unit = (x_s[b].astype(F32) - mu[b]) * scale
            w = recv4[h, :, i].reshape(C, L).astype(F32) * gin[...]
            bf[b] = bf[b] + scale * (w - mean0(w) - unit * mean0(w * unit))
            out_copy(b).start()
            return carry

        lax.fori_loop(0, NB, body, 0)

    def out_copy(b):
        return pltpu.make_async_copy(bf.at[b], out_hbm.at[:, b], out_sem.at[b])

    def line_drain(s, h, part, sibr, zs, zr, hact):
        for i in range(2):
            sib_copy(s, h, part, sibr, i).wait_send()
        for i in range(3):
            z_copy(s, h, zs, zr, i, xor(z, 1), 0).wait_send()
        for d in range(1, 4):
            ag_copy(s, h, hact, d, mine).wait_send()
        for zz in range(4):
            fw_copy(s, h, hact, zz, core).wait_send()

    def ha_copy(i):
        return pltpu.make_async_remote_copy(
            src_ref=hsend.at[0], dst_ref=hbuf_a.at[ag], send_sem=ha_s.at[i], recv_sem=ha_r.at[i],
            device_id={"agent": lax.rem(ag + i, 8), "chan": chan, "batch": batch}, device_id_type=MESH,
        )

    def hy_copy(i):
        return pltpu.make_async_remote_copy(
            src_ref=hsend.at[1], dst_ref=hbuf_y.at[y], send_sem=hy_s.at[i], recv_sem=hy_r.at[i],
            device_id=plane(lax.rem(y + i, 4) * 4 + xx), device_id_type=MESH,
        )

    def hx_copy(i):
        return pltpu.make_async_remote_copy(
            src_ref=hsend.at[2], dst_ref=hbuf_x.at[xx], send_sem=hx_s.at[i], recv_sem=hx_r.at[i],
            device_id=plane(y * 4 + lax.rem(xx + i, 4)), device_id_type=MESH,
        )

    def total(buf, n):
        out = buf[0]
        for i in range(1, n):
            out = out + buf[i]
        return out

    loads[0].wait()
    loads[1].start()

    def samples_first(first, count):
        def body(i, carry):
            piece = pl.ds(pl.multiple_of(i * CL, CL), CL)
            field = x_raw[piece].astype(F32)[:, first : first + count]
            x_s[first : first + count, piece] = jnp.transpose(field, (1, 0, 2)).astype(BF16)
            return carry

        lax.fori_loop(0, NP, body, 0)

    samples_first(0, G)
    norm_in(0, G)
    pl.semaphore_wait(barrier, NP - 1 + 7)
    send_step(0, 0, 0, send1, recv1)
    for i in range(1, NB // G):
        samples_first(i * G, G)
        norm_in(i * G, G)
        send_step(0, 0, i, send1, recv1)
    loads[2].start()
    loads[3].start()
    for h in range(1, NC):
        samples_first(h * NB, NB)
        norm_in(h * NB, NB)
        a2a_drain(0, h - 1, send1, recv1)
        a2a_send(0, h, send1, recv1)
    for load in loads[6:]:
        load.wait()
    gmid[...] = jnp.transpose(jnp.broadcast_to(gmid_ref[...], (L, C)))
    head_rows = jnp.concatenate([head_ref[...].astype(F32), jnp.zeros((8, C), F32)], axis=0)
    head16[...] = head_rows.astype(BF16)
    wide_head = jnp.concatenate([head_rows, jnp.zeros((L - 16, C), F32)], axis=0)
    headc[...] = jnp.transpose(wide_head)[:, :16].astype(BF16)
    spot = lax.broadcasted_iota(jnp.int32, (L, L), 0) == lax.rem(ord_ref[...], L)
    targets = mm(act_ref[...].astype(F32).astype(BF16), spot.astype(F32).astype(BF16))
    for b in range(B):
        tgt[b] = targets[b : b + 1, :]
    hp[...] = jnp.zeros((16, C), F32)

    loads[2].wait()
    loads[3].wait()
    for kb in range(4):
        block = slice(kb * 256, kb * 256 + 256)
        cit[block, :] = jnp.transpose(ci[:, block])
        cot[:, block] = jnp.transpose(co[block, :])
    loads[1].wait()
    loads[4].start()
    for h in range(NC):
        a2a_wait(0, h, send1, recv1)
        contract(0, h, recv1, lambda a, block: mm(a, cols(win, block)), part1, sibr1, zs1, zr1)
    for h in range(NC):
        value, slope = gelu_both(summed(0, h, zs1, zr1))
        hact1[h, mine] = value.astype(BF16)
        hslope[h] = slope
        spread(0, h, hact1)
    loads[4].wait()
    for h in range(NC):
        forward(0, h, hact1)
        gather_wait(0, h, hact1)
        expand(1, h, hact1, lambda a, group: mm(a, cols(wout, group * 2)), send2, recv2)
    for h in range(NC):
        a2a_wait(1, h, send2, recv2)
        channel_part(h)
    a2a_drain(0, NC - 1, send1, recv1)
    for h in range(NC):
        line_drain(0, h, part1, sibr1, zs1, zr1, hact1)
        a2a_drain(1, h, send2, recv2)
    hsend[0] = hp[:8]
    hbuf_a[ag] = hp[:8]
    for i in range(1, 8):
        ha_copy(i).start()
    for h in range(NC):
        a2a_wait(2, h, send3, recv3)
        contract(1, h, recv3, lambda a, block: mm_nt(a, rows(wout, block)), part2, sibr2, zs2, zr2)
    for i in range(1, 8):
        ha_copy(i).wait()
    sums = total(hbuf_a, 8)
    hsend[1] = sums
    hbuf_y[y] = sums
    for i in range(1, 4):
        hy_copy(i).start()
    for h in range(NC):
        hact2[h, mine] = (summed(1, h, zs2, zr2) * hslope[h]).astype(BF16)
        spread(1, h, hact2)
    for i in range(1, 4):
        hy_copy(i).wait()
    sums = total(hbuf_y, 4)
    hsend[2] = sums
    hbuf_x[xx] = sums
    for i in range(1, 4):
        hx_copy(i).start()
    for h in range(NC):
        forward(1, h, hact2)
        gather_wait(1, h, hact2)
        expand(3, h, hact2, lambda a, group: mm_nt(a, rows(win, group * 2)), send4, recv4)
    for i in range(1, 4):
        hx_copy(i).wait()
    hg_ref[...] = total(hbuf_x, 4)
    for h in range(NC):
        a2a_drain(2, h, send3, recv3)
        line_drain(1, h, part2, sibr2, zs2, zr2, hact2)
        if h < NC - 1:
            a2a_drain(3, h, send4, recv4)
    for h in range(NC):
        a2a_wait(3, h, send4, recv4)
        norm_back(h)

    a2a_drain(3, NC - 1, send4, recv4)
    for b in range(B):
        out_copy(b).wait()


def fused(x, gin, win, wout, gmid, ci, co, head, actions, order):
    hbm = pl.BlockSpec(memory_space=pl.ANY)
    vmem = pl.BlockSpec(memory_space=pltpu.VMEM)
    dma = pltpu.SemaphoreType.DMA
    V = pltpu.VMEM
    exchange = V((NP, B, CL, L), BF16)
    arrive = V((NC, NP, NB, CL, L), BF16)
    scratch = [
        V((1, C), F32), V((1, C), F32), V((8, C), BF16), V((B, L), jnp.int32), V((1, L), jnp.int32),
        V((C, B, L), BF16), V((B, C, L), BF16), V((T, J), BF16), V((J, T), BF16),
        V((C, K), BF16), V((K, C), BF16), V((K, C), BF16), V((C, K), BF16),
        V((C, L), F32), V((C, L), F32), V((16, C), BF16), V((C, 16), BF16),
        V((B, 1, L), F32), V((B, 1, L), F32), V((B, 1, L), F32), V((B, C, L), F32),
        exchange, exchange, exchange, exchange, arrive, arrive, arrive, arrive,
        V((NC, 2, R, 2 * Q), BF16), V((NC, 2, R, 2 * Q), BF16),
        V((NC, 2, R, 2 * Q), BF16), V((NC, 2, R, 2 * Q), BF16),
        V((NC, 3, R, Q), BF16), V((NC, 3, R, Q), BF16),
        V((NC, 3, R, Q), BF16), V((NC, 3, R, Q), BF16),
        V((NC, 8, R, Q), BF16), V((NC, 8, R, Q), BF16),
        V((2, NC, 2, R, Q), F32), V((NC, R, Q), F32),
        V((K, G * L), BF16), V((K, G * L), F32), V((K, G * L), BF16), V((16, C), F32),
        V((8, 8, C), F32), V((4, 8, C), F32), V((4, 8, C), F32), V((3, 8, C), F32),
        dma((10,)), dma((B,)), dma((4, NC)), dma((4, NC)),
        dma((2, NC, 2)), dma((2, NC, 2)), dma((2, NC, 3)), dma((2, NC, 3)),
        dma((2, NC, 3)), dma((2, NC, 3)), dma((2, NC, 4)), dma((2, NC, 4)),
        dma((8,)), dma((8,)), dma((4,)), dma((4,)), dma((4,)), dma((4,)),
    ]
    return pl.pallas_call(
        kernel,
        out_shape=(jax.ShapeDtypeStruct((C, B, L), F32), jax.ShapeDtypeStruct((8, C), F32)),
        in_specs=[pl.BlockSpec(memory_space=pltpu.HBM)] * 10,
        out_specs=(hbm, vmem),
        scratch_shapes=scratch,
        compiler_params=pltpu.CompilerParams(
            collective_id=0, has_side_effects=True, vmem_limit_bytes=46 << 20
        ),
    )(*[pltpu.with_memory_space_constraint(v, pltpu.HBM) for v in (x, gin, win, wout, gmid, ci, co, head, actions, order)])


def hand_over(grad_in, head_in, grad_out, head_out, sem):
    copies = []
    for i in range(PIECES):
        piece = pl.ds(i * (C // PIECES), C // PIECES)
        copies.append(pltpu.make_async_copy(grad_in.at[piece], grad_out.at[piece], sem.at[i]))
        copies[-1].start()
    head_out[...] = head_in[...] * (1.0 / (B * A))
    for copy in copies:
        copy.wait()


def deliver(grad, head):
    hbm = pl.BlockSpec(memory_space=pl.ANY)
    vmem = pl.BlockSpec(memory_space=pltpu.VMEM)
    return pl.pallas_call(
        hand_over,
        out_shape=(jax.ShapeDtypeStruct((C, B, L), F32), jax.ShapeDtypeStruct((8, C), F32)),
        in_specs=[hbm, vmem],
        out_specs=(hbm, vmem),
        scratch_shapes=[pltpu.SemaphoreType.DMA((PIECES,))],
        compiler_params=pltpu.CompilerParams(vmem_limit_bytes=8 << 20),
    )(grad, head)


def shards(features, norm_gain, tok_in, tok_out, mix_gain, chan_in, chan_out, head, actions, order):
    grad, head_grad = fused(
        features,
        norm_gain.reshape(1, C),
        tok_in,
        tok_out,
        mix_gain.reshape(1, C),
        chan_in,
        chan_out,
        head.T,
        actions,
        order.reshape(1, L),
    )
    grad, head_grad = deliver(grad, head_grad)
    return grad, head_grad.T


def solution(mesh):
    in_specs = (
        P(None, None, ("agent", "chan", "batch")),
        P(),
        P("agent", None),
        P(None, "agent"),
        P(),
        P(),
        P(),
        P(),
        P(None, ("agent", "chan", "batch")),
        P(("agent", "chan", "batch")),
    )
    out_specs = (P(None, None, ("agent", "chan", "batch")), P())
    return jax.shard_map(shards, mesh=mesh, in_specs=in_specs, out_specs=out_specs, check_vma=False)
```
